32 devices in a mesh: rows: 8 (over z, y), mk: 4 (over x, core).
Axes of the slice: x: 2, y: 2, z: 4, core: 2. Of those that a mesh axis runs over, the one named last changes fastest.
Arguments:
- solution_animal: float32 [6, 131072], P(None, ('rows', 'mk')), may hold values from -6 to 6
- solution_marker: float32 [6, 49152], P(None, 'mk'), may hold values from -6 to 6
- residual_animal: float32 [6, 131072], P(None, ('rows', 'mk')), may hold values from -6 to 6
- residual_marker: float32 [6, 49152], P(None, 'mk'), may hold values from -6 to 6
- direction_animal: float32 [6, 131072], P(None, ('rows', 'mk')), may hold values from -6 to 6
- direction_marker: float32 [6, 49152], P(None, 'mk'), may hold values from -6 to 6
- scaling_animal: float32 [6, 131072], P(None, ('rows', 'mk')), may hold values from 0.3 to 9, as said below
- scaling_marker: float32 [6, 49152], P(None, 'mk'), may hold values from 0.3 to 3
- previous_product: float32 [], replicated, may hold values from 943718.4 to 3932160
- genotypes: bfloat16 [3072, 49152], P('rows', 'mk'), may hold values from -0.0390625 to 0.0390625
- genetic_inverse: float32 [6, 6], replicated, may hold values from -0.28 to 4, as said below
- genomic_inverse: float32 [6, 6], replicated, may hold values from -0.28 to 4, as said below
- marker_inverse: float32 [6, 6], replicated, may hold values from -0.28 to 4, as said below
- residual_table: float32 [64, 6, 6], replicated, may hold values from -0.28 to 4, as said below
- pattern: int32 [131072], P(('rows', 'mk')), may hold values from 0 to 63
- sire_slot: int32 [131072], P(('rows', 'mk')), may hold values from 0 to 2048, as said below
- dam_slot: int32 [131072], P(('rows', 'mk')), may hold values from 0 to 2048, as said below
- genotype_row: int32 [131072], P(('rows', 'mk')), may hold values from 0 to 384, as said below
- send_list: int32 [8, 4, 8, 256], P('rows', 'mk'), may hold values from 0 to 4096, as said below
Outputs:
- next_solution_animal: float32 [6, 131072], P(None, ('rows', 'mk'))
- next_solution_marker: float32 [6, 49152], P(None, 'mk')
- next_residual_animal: float32 [6, 131072], P(None, ('rows', 'mk'))
- next_residual_marker: float32 [6, 49152], P(None, 'mk')
- reduction: float32 [], replicated
The draws below stay inside these ranges and needn't reach their ends.
Inputs may be any that keep to these rules, and one draw needn't show every extreme that they name: `send_list`: used entries are distinct local animal indices of the owner; 4096 marks an empty slot, and empty slots only follow used ones. Every device's list to itself is full, and in every column some receiving row gets full lists from all owners. `sire_slot`: points at a used slot of the parent lists sent to the animal's device, or is 8 * 256 for an unknown sire. `dam_slot`: points at a used slot of the parent lists sent to the animal's device, or is 8 * 256 for an unknown dam. `genotype_row`: within the animals of one rows block, each value below 384 occurs exactly once; 384 marks an animal without genotypes. `scaling_animal`: Positive. `genetic_inverse`: symmetric and strictly diagonally dominant with positive diagonal. `genomic_inverse`: symmetric and strictly diagonally dominant with positive diagonal. `marker_inverse`: symmetric and strictly diagonally dominant with positive diagonal. `residual_table`: entry p is symmetric, zero in the rows and columns of traits whose bit of p is 0, and strictly diagonally dominant on the others.
All inputs are finite; a program needn't handle non-finite values.
Results may differ from the reference program's by a relative error of at most 0.00045.
Values sent between devices are 32-bit elements; how exact they have to be, the bound alone decides.
No kernel may reach another device: no remote copies, remote signals or barrier semaphores. Data moves between devices by JAX's collectives and lax.ppermute only.
A program may use at most 128 MiB of HBM per device.

```python
import math
import jax
import jax.numpy as jnp
from jax import lax

TRAITS = 6
MARKERS = 49152
PATTERNS = 64
CAP = 256
NA_DEV = 4096
NG_DEV = 384
NA = 131072
NG = 3072
N_ROWS = 8
N_MK = 4


def pedigree_tables(key):
    count_key = jax.random.fold_in(key, 101)
    full_key = jax.random.fold_in(key, 102)
    stride_key = jax.random.fold_in(key, 103)
    offset_key = jax.random.fold_in(key, 104)
    counts = jax.random.randint(count_key, (N_ROWS, N_MK, N_ROWS), max(CAP // 4, 1), CAP + 1)
    self_pair = jnp.arange(N_ROWS)[:, None] == jnp.arange(N_ROWS)[None, :]
    counts = jnp.where(self_pair[:, None, :], CAP, counts)
    full_row = jax.random.randint(full_key, (N_MK,), 0, N_ROWS)
    counts = jnp.where(jnp.arange(N_ROWS)[None, None, :] == full_row[None, :, None], CAP, counts)
    primes = jnp.array([10007, 10009, 10037, 10039], jnp.int32)
    stride = primes[jax.random.randint(stride_key, counts.shape, 0, 4)]
    offset = jax.random.randint(offset_key, counts.shape, 0, NA_DEV)
    positions = jnp.arange(CAP, dtype=jnp.int32)
    local = (offset[..., None] + positions * stride[..., None]) % NA_DEV
    send_list = jnp.where(positions < counts[..., None], local, NA_DEV).astype(jnp.int32)
    return (counts.astype(jnp.int32), send_list)


def parent_slots(key, counts, salt):
    animal_index = jnp.arange(NA, dtype=jnp.int32)
    owner_row = animal_index // (N_MK * NA_DEV)
    column = animal_index // NA_DEV % N_MK
    source_row = jax.random.randint(jax.random.fold_in(key, salt), (NA,), 0, N_ROWS)
    available = counts[source_row, column, owner_row]
    source_pos = jax.random.randint(jax.random.fold_in(key, salt + 1), (NA,), 0, 1048576) % available
    known = jax.random.randint(jax.random.fold_in(key, salt + 2), (NA,), 0, 100) < 85
    return jnp.where(known, source_row * CAP + source_pos, N_ROWS * CAP).astype(jnp.int32)


def draw_send_list(key, part):
    return pedigree_tables(key)[1]


def draw_sire_slot(key, part):
    return parent_slots(key, pedigree_tables(key)[0], 7)


def draw_dam_slot(key, part):
    return parent_slots(key, pedigree_tables(key)[0], 17)


def draw_genotype_row(key, part):
    row_keys = jax.random.split(jax.random.fold_in(key, 303), N_ROWS)
    orders = jax.vmap(lambda one_key: jax.random.permutation(one_key, N_MK * NA_DEV))(row_keys)
    return jnp.where(orders < NG_DEV, orders, NG_DEV).reshape(NA).astype(jnp.int32)


def draw_scaling_animal(key, part):
    rising = 1.0 + 2.0 * jnp.arange(NA, dtype=jnp.float32) / max(NA - 1, 1)
    base = jnp.exp(jax.random.uniform(key, (TRAITS, NA), jnp.float32, math.log(0.3), math.log(3.0)))
    return base * rising[None, :]


def definite(key, count):
    diag_key = jax.random.fold_in(key, 1)
    off_key = jax.random.fold_in(key, 2)
    diagonal = jax.random.uniform(diag_key, (count, TRAITS), jnp.float32, 1.5, 3.0)
    off_part = jax.random.uniform(off_key, (count, TRAITS, TRAITS), jnp.float32, -0.25, 0.25)
    off_part = 0.5 * (off_part + jnp.swapaxes(off_part, 1, 2))
    identity = jnp.eye(TRAITS, dtype=jnp.float32)
    return off_part * (1.0 - identity) + diagonal[:, :, None] * identity


def draw_genetic_inverse(key, part):
    return definite(jax.random.fold_in(key, 501), 1)[0]


def draw_genomic_inverse(key, part):
    return definite(jax.random.fold_in(key, 502), 1)[0]


def draw_marker_inverse(key, part):
    return definite(jax.random.fold_in(key, 503), 1)[0]


def draw_residual_table(key, part):
    matrices = definite(jax.random.fold_in(key, 504), PATTERNS)
    powers = 2 ** jnp.arange(TRAITS, dtype=jnp.int32)
    observed = (jnp.arange(PATTERNS, dtype=jnp.int32)[:, None] // powers[None, :] % 2).astype(jnp.float32)
    return matrices * observed[:, :, None] * observed[:, None, :]


def plant(result, own_key, smallest, largest):
    dims = result.shape
    index_at = [jax.random.randint(jax.random.fold_in(own_key, axis), (), 0, dims[axis]) for axis in range(len(dims))]
    result = result.at[tuple(index_at)].set(smallest)
    longest = dims.index(max(dims))
    index_at[longest] = (index_at[longest] + 1) % dims[longest]
    return result.at[tuple(index_at)].set(largest)


def spiked(values, rng, source, target, blocks, factor):
    def block_of(dim):
        return (jnp.arange(values.shape[dim]) // (values.shape[dim] // blocks)).reshape((-1,) + (1,) * (values.ndim - 1 - dim))

    near = jax.random.permutation(rng, blocks)[block_of(target)]
    other_side = (block_of(target) + blocks // 2) % blocks
    return jnp.where((block_of(source) == near) | (block_of(source) == other_side), factor * values, values)


def block_levels(key, shape, shards, least, top_value):
    gain, own = 1.0, jax.random.fold_in(key, 6)
    for dim, blocks in shards:
        steps = jnp.exp(jax.random.uniform(jax.random.fold_in(own, dim), (blocks,), jnp.float32, least / len(shards), top_value / len(shards)))
        gain = gain * jnp.repeat(steps, shape[dim] // blocks).reshape([-1 if axis == dim else 1 for axis in range(len(shape))])
    return gain


def centred(stream_key, extent, width, bound, pieces=(), kind=jnp.bfloat16):
    values = width * jax.random.normal(stream_key, extent, jnp.float32)
    if pieces:
        values = values * block_levels(stream_key, extent, pieces, -0.22, 0.18)
    return jnp.clip(values, -bound, bound).astype(kind)


def noise_with(stream_key, shape, scale, reach, cuts, heavy, kind=jnp.bfloat16):
    values = scale * jax.random.normal(stream_key, shape, jnp.float32)
    if cuts:
        values = values * block_levels(stream_key, shape, cuts, -0.22, 0.18)
    return jnp.clip(spiked(values, jax.random.fold_in(stream_key, 3), *heavy), -reach, reach).astype(kind)


def setup_inputs(seed: int = 0) -> dict:
    key_list = jax.random.split(jax.random.key(seed), 20)
    solution_animal = centred(key_list[0], (TRAITS, NA), 1.0, 6.0, ((1, 32),), jnp.float32)
    solution_marker = centred(key_list[1], (TRAITS, MARKERS), 1.0, 6.0, ((1, 4),), jnp.float32)
    residual_animal = centred(key_list[2], (TRAITS, NA), 1.0, 6.0, ((1, 32),), jnp.float32)
    residual_marker = centred(key_list[3], (TRAITS, MARKERS), 1.0, 6.0, ((1, 4),), jnp.float32)
    direction_animal = centred(key_list[4], (TRAITS, NA), 1.0, 6.0, ((1, 32),), jnp.float32)
    direction_marker = centred(key_list[5], (TRAITS, MARKERS), 1.0, 6.0, ((1, 4),), jnp.float32)
    scaling_animal = draw_scaling_animal(jax.random.fold_in(key_list[19], 71), 0)
    scaling_marker = jnp.clip(jnp.exp(math.log(3.0) - 2.3025851 * jax.random.uniform(key_list[7], (TRAITS, MARKERS), jnp.float32) ** block_levels(key_list[7], (TRAITS, MARKERS), ((1, 4),), -0.2, 0.2)), 0.3, 3.0)
    previous_product = jnp.clip(jnp.exp(jax.random.uniform(key_list[8], (), jnp.float32, math.log(943718.4), math.log(3932160))), 943718.4, 3932160)
    genotypes = noise_with(key_list[9], (NG, MARKERS), MARKERS ** -0.5, 0.0390625, ((0, 8), (1, 4)), (0, 1, 8, 2.0))
    genetic_inverse = draw_genetic_inverse(jax.random.fold_in(key_list[19], 71), 0)
    genomic_inverse = draw_genomic_inverse(jax.random.fold_in(key_list[19], 71), 0)
    marker_inverse = draw_marker_inverse(jax.random.fold_in(key_list[19], 71), 0)
    residual_table = draw_residual_table(jax.random.fold_in(key_list[19], 71), 0)
    pattern = plant(jax.random.randint(key_list[14], (NA,), 0, PATTERNS), jax.random.fold_in(key_list[14], 1), 0, PATTERNS - 1).astype(jnp.int32)
    sire_slot = draw_sire_slot(jax.random.fold_in(key_list[19], 71), 0)
    dam_slot = draw_dam_slot(jax.random.fold_in(key_list[19], 71), 0)
    genotype_row = draw_genotype_row(jax.random.fold_in(key_list[19], 71), 0)
    send_list = draw_send_list(jax.random.fold_in(key_list[19], 71), 0)
    return dict(solution_animal=solution_animal, solution_marker=solution_marker, residual_animal=residual_animal, residual_marker=residual_marker, direction_animal=direction_animal, direction_marker=direction_marker, scaling_animal=scaling_animal, scaling_marker=scaling_marker, previous_product=previous_product, genotypes=genotypes, genetic_inverse=genetic_inverse, genomic_inverse=genomic_inverse, marker_inverse=marker_inverse, residual_table=residual_table, pattern=pattern, sire_slot=sire_slot, dam_slot=dam_slot, genotype_row=genotype_row, send_list=send_list)


precise = lax.Precision.HIGHEST


def parent_global(slot_list, send_list, column, owner_row):
    slot_total = N_ROWS * CAP
    source_row = jnp.minimum(slot_list // CAP, N_ROWS - 1).astype(jnp.int32)
    source_pos = (slot_list % CAP).astype(jnp.int32)
    local = send_list[source_row, column, owner_row, source_pos]
    known = slot_list < slot_total
    parent = jnp.where(known, (source_row * N_MK + column) * NA_DEV + local, NA).astype(jnp.int32)
    return parent, known


def reference(solution_animal, solution_marker, residual_animal, residual_marker, direction_animal, direction_marker, scaling_animal, scaling_marker, previous_product, genotypes, genetic_inverse, genomic_inverse, marker_inverse, residual_table, pattern, sire_slot, dam_slot, genotype_row, send_list):
    animal_index = jnp.arange(NA, dtype=jnp.int32)
    owner_row = (animal_index // (N_MK * NA_DEV)).astype(jnp.int32)
    column = ((animal_index // NA_DEV) % N_MK).astype(jnp.int32)
    sire, sire_known = parent_global(sire_slot, send_list, column, owner_row)
    dam, dam_known = parent_global(dam_slot, send_list, column, owner_row)
    known = sire_known.astype(jnp.float32) + dam_known.astype(jnp.float32)
    mendel = 1.0 / (1.0 - 0.25 * known)
    search_animal = scaling_animal * residual_animal
    search_marker = scaling_marker * residual_marker
    product_now = jnp.sum(residual_animal * search_animal) + jnp.sum(residual_marker * search_marker)
    norm_before = jnp.sum(residual_animal * residual_animal) + jnp.sum(residual_marker * residual_marker)
    conjugacy = product_now / previous_product
    new_animal = search_animal + conjugacy * direction_animal
    new_marker = search_marker + conjugacy * direction_marker
    padded = jnp.concatenate([new_animal, jnp.zeros((TRAITS, 1), jnp.float32)], axis=1)
    sampling = mendel[None, :] * (new_animal - 0.5 * padded[:, sire] - 0.5 * padded[:, dam])
    spread = jnp.zeros((TRAITS, NA + 1), jnp.float32)
    spread = spread.at[:, sire].add(-0.5 * sampling).at[:, dam].add(-0.5 * sampling)
    pedigree = sampling + spread[:, :NA]
    global_row = jnp.where(genotype_row < NG_DEV, owner_row * NG_DEV + genotype_row, NG).astype(jnp.int32)
    placed = jnp.zeros((TRAITS, NG + 1), jnp.float32).at[:, global_row].add(new_animal)[:, :NG]
    predicted = lax.dot_general(new_marker.astype(jnp.bfloat16), genotypes, (((1,), (1,)), ((), ())), preferred_element_type=jnp.float32)
    deviation = jnp.dot(genomic_inverse, placed - predicted, precision=precise)
    genomic_term = jnp.concatenate([deviation, jnp.zeros((TRAITS, 1), jnp.float32)], axis=1)[:, global_row]
    blocks = residual_table[pattern]
    record_term = jnp.einsum("nts,sn->tn", blocks, new_animal, precision=precise)
    image_animal = jnp.dot(genetic_inverse, pedigree, precision=precise) + record_term + genomic_term
    marker_terms = lax.dot_general(deviation.astype(jnp.bfloat16), genotypes, (((1,), (0,)), ((), ())), preferred_element_type=jnp.float32)
    image_marker = jnp.dot(marker_inverse, new_marker, precision=precise) - marker_terms
    curvature = jnp.sum(new_animal * image_animal) + jnp.sum(new_marker * image_marker)
    step_size = product_now / curvature
    next_solution_animal = solution_animal + step_size * new_animal
    next_solution_marker = solution_marker + step_size * new_marker
    next_residual_animal = residual_animal - step_size * image_animal
    next_residual_marker = residual_marker - step_size * image_marker
    norm_after = jnp.sum(next_residual_animal * next_residual_animal) + jnp.sum(next_residual_marker * next_residual_marker)
    reduction = norm_after / norm_before
    return next_solution_animal, next_solution_marker, next_residual_animal, next_residual_marker, reduction
```

```python
import functools

import jax
import jax.numpy as jnp
from jax import lax
from jax.experimental import pallas as pl
from jax.experimental.pallas import tpu as pltpu
from jax.sharding import PartitionSpec as P

F32 = jnp.float32
BF16 = jnp.bfloat16
PAD = 8
LANES = 128


def shape_of(*dims, dtype=F32):
    return jax.ShapeDtypeStruct(dims, dtype)


def call(kernel, out_shape, scratch=(), **options):
    return pl.pallas_call(kernel, out_shape=out_shape, scratch_shapes=list(scratch), **options)


def parts_of(values):
    high = values.astype(BF16).astype(F32)
    rest = values - high
    middle = rest.astype(BF16).astype(F32)
    return jnp.concatenate([high, middle, rest - middle], axis=0)


def add_parts(stacked):
    return stacked[:PAD] + stacked[PAD : 2 * PAD] + stacked[2 * PAD :]


ROWS_EACH = 3 * PAD


def one_hot(low, base):
    wanted = lax.broadcasted_iota(jnp.int32, (base, low.shape[1]), 0)
    return jnp.where(wanted == low, 1.0, 0.0).astype(BF16)


def dot(left, right):
    return lax.dot_general(left, right, (((1,), (0,)), ((), ())), preferred_element_type=F32)


def dot_t(left, right):
    return lax.dot_general(left, right, (((1,), (1,)), ((), ())), preferred_element_type=F32)


def select_blocks(products, high, first, count):
    total = None
    for h in range(count):
        block = add_parts(products[h * ROWS_EACH : (h + 1) * ROWS_EACH])
        block = jnp.where(high == first + h, block, 0.0)
        total = block if total is None else total + block
    return total


def masked_blocks(stacked, high, first, count):
    return jnp.concatenate(
        [jnp.where(high == first + h, stacked, 0.0) for h in range(count)], axis=0
    ).astype(BF16)


def fold(values):
    total = values[:, :LANES]
    for start in range(LANES, values.shape[1], LANES):
        total = total + values[:, start : start + LANES]
    return total


def load_matrix(matrix_ref, padded_ref):
    padded_ref[...] = jnp.zeros_like(padded_ref)
    size = matrix_ref.shape[0]
    padded_ref[:size, :size] = matrix_ref[...]


def apply_matrix(padded_ref, values, count):
    total = None
    for s in range(count):
        term = padded_ref[:, s : s + 1] * values[s : s + 1, :]
        total = term if total is None else total + term
    return total


def total_of(tile):
    return jnp.sum(jnp.sum(tile, axis=0, keepdims=True), axis=1, keepdims=True)


def sums_of(received_ref):
    tile = received_ref[0]
    for i in range(1, received_ref.shape[0]):
        tile = tile + received_ref[i]
    return tile


def product_of(sums_ref):
    return jnp.sum(sums_of(sums_ref)[0:1], axis=1, keepdims=True)


def norm_of(sums_ref):
    return jnp.sum(sums_of(sums_ref)[1:2], axis=1, keepdims=True)


def totals_kernel(marker_weight, res_a, scal_a, res_m, scal_m, out):
    def pair(res_ref, scal_ref):
        res = res_ref[...]
        square = res * res
        return (
            jnp.sum(fold(square * scal_ref[...]), axis=0, keepdims=True),
            jnp.sum(fold(square), axis=0, keepdims=True),
        )

    product_a, norm_a = pair(res_a, scal_a)
    product_m, norm_m = pair(res_m, scal_m)
    row = lax.broadcasted_iota(jnp.int32, (PAD, LANES), 0)
    product = product_a + marker_weight * product_m
    norm = norm_a + marker_weight * norm_m
    tile = jnp.where(row == 0, product, jnp.where(row == 1, norm, 0.0))
    out[...] = jnp.broadcast_to(tile[None], out.shape)


def animal_kernel(bits, sums, previous, res, scal, direction, send, new_ref, out):
    traits, animals = res.shape
    base = 1 << bits
    conjugacy = product_of(sums) / previous[...]
    new_ref[...] = jnp.zeros_like(new_ref)
    new_ref[:traits] = scal[...] * res[...] + conjugacy * direction[...]
    blocks = animals // base
    table = jnp.concatenate(
        [parts_of(new_ref[:, h * base : (h + 1) * base]) for h in range(blocks)], axis=0
    ).astype(BF16)

    def one(r):
        index = send[pl.ds(r, 1), :]
        products = dot(table, one_hot(index & (base - 1), base))
        out[r] = select_blocks(products, index >> bits, 0, blocks)

    if send.shape[0] <= 8:
        for r in range(send.shape[0]):
            one(r)
    else:
        pl.loop(0, send.shape[0])(one)


def predict_kernel(
    bits,
    sums,
    previous,
    res,
    scal,
    direction,
    genotypes,
    new_a,
    row_index,
    new_m,
    placed_ref,
    out,
    conjugacy_ref,
    total_ref,
):
    step = pl.program_id(0)
    traits = res.shape[0]
    genotyped = genotypes.shape[0]
    base = 1 << bits

    @pl.when(step == 0)
    def _():
        conjugacy_ref[...] = jnp.broadcast_to(product_of(sums) / previous[...], (PAD, LANES))
        total_ref[...] = jnp.zeros_like(total_ref)
        blocks = -(-genotyped // base)
        width = 1024
        total = jnp.zeros((blocks * ROWS_EACH, base), F32)
        for start in range(0, new_a.shape[1], width):
            index = row_index[:, start : start + width]
            stacked = parts_of(new_a[:, start : start + width])
            total = total + dot_t(
                masked_blocks(stacked, index >> bits, 0, blocks),
                one_hot(index & (base - 1), base),
            )
        for h in range(blocks):
            size = min(base, genotyped - h * base)
            block = add_parts(total[h * ROWS_EACH : (h + 1) * ROWS_EACH])
            placed_ref[:, h * base : h * base + size] = block[:, :size]

    new_m[...] = jnp.zeros_like(new_m)
    new_m[:traits] = scal[...] * res[...] + conjugacy_ref[:traits, 0:1] * direction[...]
    total_ref[...] += dot_t(new_m[...].astype(BF16), genotypes[...])

    @pl.when(step == pl.num_programs(0) - 1)
    def _():
        out[...] = jnp.broadcast_to((placed_ref[...] - total_ref[...])[None], out.shape)


def pedigree_kernel(
    bits,
    parents,
    new_a,
    sire,
    dam,
    pattern,
    table,
    genetic,
    base_ref,
    back_ref,
    part_ref,
    left_ref,
    matrix_ref,
):
    owners, _, base = parents.shape
    traits = genetic.shape[0]
    patterns = table.shape[1]
    animals = new_a.shape[1]
    load_matrix(genetic, matrix_ref)
    for h in range(0, owners, 2):
        left_ref[h * ROWS_EACH : (h + 2) * ROWS_EACH, :] = jnp.concatenate(
            [parts_of(parents[h]), parts_of(parents[h + 1])], axis=0
        ).astype(BF16)
    values = table[...]
    high_part = values.astype(BF16).astype(F32)
    rest = values - high_part
    middle_part = rest.astype(BF16).astype(F32)
    record_table = jnp.concatenate([high_part, middle_part, rest - middle_part], axis=0).astype(
        BF16
    )
    group = min(8, owners)
    groups = owners // group

    def over_groups(body):
        for g in range(groups):
            body(g)

    gathered_ref = base_ref
    width = 1024
    back_ref[...] = jnp.zeros_like(back_ref)
    part = jnp.zeros((PAD, LANES), F32)
    for start in range(0, animals, width):
        window = slice(start, start + width)
        new = new_a[:, window]
        sire_index, dam_index = sire[:, window], dam[:, window]
        sire_high, dam_high = sire_index >> bits, dam_index >> bits
        sire_hot = one_hot(sire_index & (base - 1), base)
        dam_hot = one_hot(dam_index & (base - 1), base)
        gathered_ref[:, window] = jnp.zeros((PAD, width), F32)

        def gather(g):
            left = left_ref[pl.ds(g * group * ROWS_EACH, group * ROWS_EACH), :]
            gathered_ref[:, window] += select_blocks(
                dot(left, sire_hot), sire_high, g * group, group
            ) + select_blocks(dot(left, dam_hot), dam_high, g * group, group)

        over_groups(gather)
        slots = owners * base
        known = (sire_index < slots).astype(F32) + (dam_index < slots).astype(F32)
        mendel = 1.0 / (1.0 - 0.25 * known)
        difference = new - 0.5 * gathered_ref[:, window]
        sampling = mendel * difference
        genetic_term = apply_matrix(matrix_ref, sampling, traits)
        blocks = dot(record_table, one_hot(pattern[:, window], patterns))
        record = None
        size = traits * PAD
        for s in range(traits):
            row = slice(s * PAD, (s + 1) * PAD)
            block = blocks[row] + blocks[size:][row] + blocks[2 * size :][row]
            term = block * new[s : s + 1, :]
            record = term if record is None else record + term
        base_ref[:, window] = genetic_term + record
        part = part + fold(difference * genetic_term + new * record)
        stacked = parts_of(-0.5 * sampling)

        def scatter(g):
            total = dot_t(masked_blocks(stacked, sire_high, g * group, group), sire_hot) + dot_t(
                masked_blocks(stacked, dam_high, g * group, group), dam_hot
            )
            for h in range(group):
                back_ref[g * group + h] += add_parts(total[h * ROWS_EACH : (h + 1) * ROWS_EACH])

        over_groups(scatter)
    part_ref[...] = part


def deviation_kernel(
    share,
    differences,
    placed,
    genomic,
    marker_inverse,
    genotypes,
    new_m,
    back,
    part,
    deviation_ref,
    out,
    genomic_ref,
    marker_ref,
    total_ref,
):
    step = pl.program_id(0)
    traits = genomic.shape[0]
    owners = out.shape[0]
    capacity = back.shape[2]
    padded = out.shape[2] - capacity - LANES

    @pl.when(step == 0)
    def _():
        load_matrix(genomic, genomic_ref)
        load_matrix(marker_inverse, marker_ref)
        deviation = apply_matrix(genomic_ref, sums_of(differences), traits)
        deviation_ref[...] = deviation
        total_ref[...] = part[...] + fold(placed[...] * deviation)
        out[:, :, padded : padded + capacity] = back[...]

    new = new_m[...]
    terms = dot(deviation_ref[...].astype(BF16), genotypes[...])
    per_step = new.shape[1] // share
    for j in range(per_step):
        out[step * per_step + j, :, :share] = terms[:, j * share : (j + 1) * share]
    image = apply_matrix(marker_ref, new, traits)
    total_ref[...] += fold(new * (image * (1.0 / owners) - terms))

    @pl.when(step == pl.num_programs(0) - 1)
    def _():
        out[:, :, padded + capacity :] = jnp.broadcast_to(total_ref[...][None], (owners, PAD, LANES))


def spread_kernel(received, out):
    start = received.shape[2] - LANES
    tile = received[0, :, start:]
    for i in range(1, received.shape[0]):
        tile = tile + received[i, :, start:]
    out[...] = jnp.broadcast_to(tile[None], out.shape)


def image_kernel(
    bits, received, send, base_image, deviation, row_index, genetic, out, matrix_ref, table_ref
):
    owners = received.shape[0]
    base = 1 << bits
    traits = genetic.shape[0]
    animals = base_image.shape[1]
    genotyped = deviation.shape[1]
    start = received.shape[2] - LANES - base
    load_matrix(genetic, matrix_ref)
    blocks = animals // base

    def scatter(r, total):
        index = send[pl.ds(r, 1), :]
        stacked = parts_of(received[r, :, start : start + base])
        return total + dot_t(
            masked_blocks(stacked, index >> bits, 0, blocks), one_hot(index & (base - 1), base)
        )

    total = jnp.zeros((blocks * ROWS_EACH, base), F32)
    if owners <= 8:
        for r in range(owners):
            total = scatter(r, total)
    else:
        total = lax.fori_loop(0, owners, scatter, total)
    table_ref[...] = jnp.zeros_like(table_ref)
    table_ref[:, :genotyped] = deviation[...]
    places = table_ref.shape[1] // base
    table = jnp.concatenate(
        [parts_of(table_ref[:, h * base : (h + 1) * base]) for h in range(places)], axis=0
    ).astype(BF16)
    for h in range(blocks):
        window = slice(h * base, (h + 1) * base)
        index = row_index[:, window]
        gathered = add_parts(total[h * ROWS_EACH : (h + 1) * ROWS_EACH])
        genomic_term = select_blocks(
            dot(table, one_hot(index & (base - 1), base)), index >> bits, 0, places
        )
        out[:, window] = (
            base_image[:, window] + apply_matrix(matrix_ref, gathered, traits) + genomic_term
        )


def step_of(sums, curvature):
    return product_of(sums) / total_of(sums_of(curvature))


def update_kernel(
    row,
    share,
    sums,
    curvature,
    sol_a,
    res_a,
    new_a,
    image_a,
    received,
    new_share,
    res_share,
    marker_inverse,
    next_sol_a,
    next_res_a,
    out,
    matrix_ref,
):
    del row
    traits = sol_a.shape[0]
    owners = out.shape[0]
    step = step_of(sums, curvature)
    next_sol_a[...] = sol_a[...] + step * new_a[:traits]
    next_animal = res_a[...] - step * image_a[:traits]
    next_res_a[...] = next_animal
    load_matrix(marker_inverse, matrix_ref)
    terms = received[0, :, :share]
    for i in range(1, owners):
        terms = terms + received[i, :, :share]
    image = apply_matrix(matrix_ref, new_share[...], traits) - terms
    next_share = res_share[...] - step * image[:traits]
    square = next_share * next_share
    edge = share - share % LANES
    part = jnp.sum(fold(next_animal * next_animal), axis=0, keepdims=True)
    if edge:
        part = part + jnp.sum(fold(square[:, :edge]), axis=0, keepdims=True)
    if edge < share:
        rest = jnp.sum(jnp.sum(square[:, edge:], axis=1, keepdims=True), axis=0, keepdims=True)
        part = part + jnp.where(lax.broadcasted_iota(jnp.int32, (1, LANES), 1) == 0, rest, 0.0)
    norm_row = lax.broadcasted_iota(jnp.int32, (PAD, LANES), 0) == 0
    tile = jnp.where(norm_row, part, 0.0)
    padded = out.shape[2] - LANES
    for i in range(owners):
        out[i] = jnp.zeros(out.shape[1:], F32)
        out[i, :traits, :share] = next_share
        out[i, :, padded:] = tile


def marker_solution_kernel(sums, curvature, sol, new, out):
    out[...] = sol[...] + step_of(sums, curvature) * new[: sol.shape[0]]


def collect_kernel(share, received, next_res, out):
    traits = next_res.shape[0]
    padded = received.shape[2] - LANES
    tile = received[0, :, padded:]
    for i in range(received.shape[0]):
        next_res[:, i * share : (i + 1) * share] = received[i, :traits, :share]
        if i:
            tile = tile + received[i, :, padded:]
    out[...] = jnp.broadcast_to(tile[None], out.shape)


def reduction_kernel(sums, norms, out):
    out[...] = total_of(sums_of(norms)) / norm_of(sums)


def exchange(values, axes):
    return lax.all_to_all(values, axes, split_axis=0, concat_axis=0, tiled=True)


def local(
    solution_animal,
    solution_marker,
    residual_animal,
    residual_marker,
    direction_animal,
    direction_marker,
    scaling_animal,
    scaling_marker,
    previous_product,
    genotypes,
    genetic_inverse,
    genomic_inverse,
    marker_inverse,
    residual_table,
    pattern,
    sire_slot,
    dam_slot,
    genotype_row,
    send_list,
):
    traits, animals = residual_animal.shape
    markers = residual_marker.shape[1]
    genotyped = genotypes.shape[0]
    rows = lax.axis_size("rows")
    columns = lax.axis_size("mk")
    capacity = send_list.shape[3]
    bits = capacity.bit_length() - 1
    share = markers // rows
    padded = -(-share // LANES) * LANES
    chunk = share * max(1, 1536 // share)
    steps = markers // chunk
    patterns = residual_table.shape[0]
    row = lax.axis_index("rows").astype(jnp.int32).reshape(1)
    previous = previous_product.reshape(1, 1)
    send = send_list.reshape(rows, capacity)
    sire, dam = sire_slot.reshape(1, animals), dam_slot.reshape(1, animals)
    kinds, places = pattern.reshape(1, animals), genotype_row.reshape(1, animals)
    table = jnp.pad(jnp.transpose(residual_table, (2, 1, 0)), ((0, 0), (0, PAD - traits), (0, 0)))
    table = table.reshape(traits * PAD, patterns)

    sums = exchange(
        call(
            functools.partial(totals_kernel, 1.0 / rows),
            shape_of(rows * columns, PAD, LANES),
            name="totals",
        )(residual_animal, scaling_animal, residual_marker, scaling_marker),
        ("rows", "mk"),
    )
    new_animal, outgoing = call(
        functools.partial(animal_kernel, bits),
        (shape_of(PAD, animals), shape_of(rows, PAD, capacity)),
        name="animals",
    )(sums, previous, residual_animal, scaling_animal, direction_animal, send)
    parents = exchange(outgoing, "rows")

    def fixed(array):
        return pl.BlockSpec(array.shape, lambda k, n=len(array.shape): (0,) * n)

    def moving(height):
        return pl.BlockSpec((height, chunk), lambda k: (0, k))

    new_marker, placed, difference = call(
        functools.partial(predict_kernel, bits),
        (shape_of(PAD, markers), shape_of(PAD, genotyped), shape_of(columns, PAD, genotyped)),
        (pltpu.VMEM((PAD, LANES), F32), pltpu.VMEM((PAD, genotyped), F32)),
        grid=(steps,),
        in_specs=[
            fixed(sums),
            fixed(previous),
            moving(traits),
            moving(traits),
            moving(traits),
            moving(genotyped),
            fixed(new_animal),
            fixed(places),
        ],
        out_specs=(
            moving(PAD),
            fixed(shape_of(PAD, genotyped)),
            fixed(shape_of(columns, PAD, genotyped)),
        ),
        name="predict",
    )(
        sums,
        previous,
        residual_marker,
        scaling_marker,
        direction_marker,
        genotypes,
        new_animal,
        places,
    )
    differences = exchange(difference, "mk")
    base_image, back, part = call(
        functools.partial(pedigree_kernel, bits),
        (shape_of(PAD, animals), shape_of(rows, PAD, capacity), shape_of(PAD, LANES)),
        (pltpu.VMEM((rows * ROWS_EACH, capacity), BF16), pltpu.VMEM((PAD, LANES), F32)),
        name="pedigree",
    )(parents, new_animal, sire, dam, kinds, table, genetic_inverse)
    out_shape = shape_of(rows, PAD, padded + capacity + LANES)
    deviation, payload = call(
        functools.partial(deviation_kernel, share),
        (shape_of(PAD, genotyped), out_shape),
        (pltpu.VMEM((PAD, LANES), F32),) * 3,
        grid=(steps,),
        in_specs=[
            fixed(differences),
            fixed(placed),
            fixed(genomic_inverse),
            fixed(marker_inverse),
            moving(genotyped),
            moving(PAD),
            fixed(back),
            fixed(part),
        ],
        out_specs=(fixed(placed), fixed(out_shape)),
        name="deviation",
    )(differences, placed, genomic_inverse, marker_inverse, genotypes, new_marker, back, part)
    received = exchange(payload, "rows")
    curvature = exchange(
        call(spread_kernel, shape_of(columns, PAD, LANES), name="spread")(received), "mk"
    )
    table_width = -(-genotyped // capacity) * capacity
    image_animal = call(
        functools.partial(image_kernel, bits),
        shape_of(PAD, animals),
        (pltpu.VMEM((PAD, LANES), F32), pltpu.VMEM((PAD, table_width), F32)),
        name="image",
    )(received, send, base_image, deviation, places, genetic_inverse)

    if share % LANES:
        start = row[0] * share
        new_share = lax.dynamic_slice_in_dim(new_marker, start, share, 1)
        res_share = lax.dynamic_slice_in_dim(residual_marker, start, share, 1)

        def own(height):
            return pl.BlockSpec((height, share), lambda k, r: (0, 0))
    else:
        new_share, res_share = new_marker, residual_marker

        def own(height):
            return pl.BlockSpec((height, share), lambda k, r: (0, r[0]))

    def still(array):
        return pl.BlockSpec(array.shape, lambda k, r, n=len(array.shape): (0,) * n)

    out_shape = shape_of(rows, PAD, padded + LANES)
    next_solution_animal, next_residual_animal, payload = pl.pallas_call(
        lambda r, *refs: update_kernel(r, share, *refs),
        out_shape=(shape_of(traits, animals), shape_of(traits, animals), out_shape),
        grid_spec=pltpu.PrefetchScalarGridSpec(
            num_scalar_prefetch=1,
            grid=(1,),
            in_specs=[
                still(sums),
                still(curvature),
                still(solution_animal),
                still(residual_animal),
                still(new_animal),
                still(image_animal),
                still(received),
                own(PAD),
                own(traits),
                still(marker_inverse),
            ],
            out_specs=(still(solution_animal), still(solution_animal), still(out_shape)),
            scratch_shapes=[pltpu.VMEM((PAD, LANES), F32)],
        ),
        name="update",
    )(
        row,
        sums,
        curvature,
        solution_animal,
        residual_animal,
        new_animal,
        image_animal,
        received,
        new_share,
        res_share,
        marker_inverse,
    )
    gathered = exchange(payload, "rows")
    next_solution_marker = call(
        marker_solution_kernel, shape_of(traits, markers), name="marker_solution"
    )(sums, curvature, solution_marker, new_marker)
    next_residual_marker, norm = call(
        functools.partial(collect_kernel, share),
        (shape_of(traits, markers), shape_of(columns, PAD, LANES)),
        name="collect",
    )(gathered)
    reduction = call(reduction_kernel, shape_of(1, 1), name="reduction")(
        sums, exchange(norm, "mk")
    ).reshape(())
    return (
        next_solution_animal,
        next_solution_marker,
        next_residual_animal,
        next_residual_marker,
        reduction,
    )


def solution(mesh):
    animal, marker = P(None, ("rows", "mk")), P(None, "mk")
    index = P(("rows", "mk"))
    return jax.shard_map(
        local,
        mesh=mesh,
        in_specs=(
            animal,
            marker,
            animal,
            marker,
            animal,
            marker,
            animal,
            marker,
            P(),
            P("rows", "mk"),
            P(),
            P(),
            P(),
            P(),
            index,
            index,
            index,
            index,
            P("rows", "mk", None, None),
        ),
        out_specs=(animal, marker, animal, marker, P()),
        check_vma=False,
    )
```

```python
import functools

import jax
import jax.numpy as jnp
from jax import lax
from jax.experimental import pallas as pl
from jax.experimental.pallas import tpu as pltpu
from jax.sharding import PartitionSpec as P

F32 = jnp.float32
BF16 = jnp.bfloat16
PAD = 8
LANES = 128


def shape_of(*dims, dtype=F32):
    return jax.ShapeDtypeStruct(dims, dtype)


def call(kernel, out_shape, scratch=(), **options):
    return pl.pallas_call(kernel, out_shape=out_shape, scratch_shapes=list(scratch), **options)


def parts_of(values):
    high = values.astype(BF16).astype(F32)
    rest = values - high
    middle = rest.astype(BF16).astype(F32)
    return jnp.concatenate([high, middle, rest - middle], axis=0)


def add_parts(stacked):
    return stacked[:PAD] + stacked[PAD : 2 * PAD] + stacked[2 * PAD :]


ROWS_EACH = 3 * PAD


def one_hot(low, base):
    wanted = lax.broadcasted_iota(jnp.int32, (base, low.shape[1]), 0)
    return jnp.where(wanted == low, 1.0, 0.0).astype(BF16)


def dot(left, right):
    return lax.dot_general(left, right, (((1,), (0,)), ((), ())), preferred_element_type=F32)


def dot_t(left, right):
    return lax.dot_general(left, right, (((1,), (1,)), ((), ())), preferred_element_type=F32)


def select_blocks(products, high, first, count):
    total = None
    for h in range(count):
        block = add_parts(products[h * ROWS_EACH : (h + 1) * ROWS_EACH])
        block = jnp.where(high == first + h, block, 0.0)
        total = block if total is None else total + block
    return total


def masked_blocks(stacked, high, first, count):
    return jnp.concatenate(
        [jnp.where(high == first + h, stacked, 0.0) for h in range(count)], axis=0
    ).astype(BF16)


def fold(values):
    total = values[:, :LANES]
    for start in range(LANES, values.shape[1], LANES):
        total = total + values[:, start : start + LANES]
    return total


def load_matrix(matrix_ref, padded_ref):
    padded_ref[...] = jnp.zeros_like(padded_ref)
    size = matrix_ref.shape[0]
    padded_ref[:size, :size] = matrix_ref[...]


def apply_matrix(padded_ref, values, count):
    total = None
    for s in range(count):
        term = padded_ref[:, s : s + 1] * values[s : s + 1, :]
        total = term if total is None else total + term
    return total


def sums_of(received_ref):
    tile = received_ref[0]
    for i in range(1, received_ref.shape[0]):
        tile = tile + received_ref[i]
    return tile


def product_of(sums_ref):
    return jnp.sum(sums_of(sums_ref)[0:1], axis=1, keepdims=True)


def norm_of(sums_ref):
    return jnp.sum(sums_of(sums_ref)[1:2], axis=1, keepdims=True)


def two_sum(left, right):
    total = left + right
    back = total - left
    return total, (left - (total - back)) + (right - back)


def halves(values):
    scaled = values * 4097.0
    high = scaled - (scaled - values)
    return high, values - high


def two_product(left, left_halves, right, right_halves):
    product = left * right
    (lh, ll), (rh, rl) = left_halves, right_halves
    return product, ((lh * rh - product) + lh * rl + ll * rh) + ll * rl


def exact_sums(pairs):
    columns = []
    for left, right in pairs:
        lh, rh = halves(left), halves(right)
        for a, ah, b, bh in ((left, lh, left, lh), (left, lh, right, rh), (right, rh, right, rh)):
            columns.append(two_product(a, ah, b, bh))
    results = []
    for kind in range(3):
        total = error = None
        for product, rounding in columns[kind::3]:
            for start in range(0, product.shape[1], LANES):
                window = slice(start, start + LANES)
                if total is None:
                    total, error = product[:, window], rounding[:, window]
                else:
                    total, extra = two_sum(total, product[:, window])
                    error = error + (extra + rounding[:, window])
        row, rest = total[0:1], error[0:1]
        for t in range(1, total.shape[0]):
            row, extra = two_sum(row, total[t : t + 1])
            rest = rest + (extra + error[t : t + 1])
        results += [row, rest]
    return results


def rows_tile(rows):
    place = lax.broadcasted_iota(jnp.int32, (PAD, LANES), 0)
    tile = jnp.zeros((PAD, LANES), F32)
    for k, row in enumerate(rows):
        tile = jnp.where(place == k, row, tile)
    return tile


def exact_tile(tiles):
    total = tiles[0]
    error = jnp.zeros_like(total)
    for tile in tiles[1:]:
        total, extra = two_sum(total, tile)
        error = error + extra
    place = lax.broadcasted_iota(jnp.int32, (PAD, LANES), 0)
    errors = (place == 2) | (place == 4) | (place == 6)
    return total + jnp.where(errors, pltpu.roll(error, 1, 0), 0.0)


def is_packed(traits, share):
    return traits == 6 and share % (4 * LANES) == 0


def packed_width(traits, share):
    return share * 3 // 4 if is_packed(traits, share) else -(-share // LANES) * LANES


def spare_pieces(traits, share):
    main, rest = share * 3 // 4, share // 4
    return [
        (t, main, rest, traits + t // 3, t % 3 * rest)
        for t in range(traits if is_packed(traits, share) else 0)
    ]


def pack(out, i, values, traits, share):
    if not is_packed(traits, share):
        out[i, :, :share] = values
        return
    main = share * 3 // 4
    out[i, :traits, :main] = values[:traits, :main]
    for t, start, width, row, column in spare_pieces(traits, share):
        out[i, row : row + 1, column : column + width] = values[t : t + 1, start : start + width]


def totals_kernel(marker_weight, res_a, scal_a, res_m, scal_m, out, token):
    def pair(res_ref, scal_ref):
        res = res_ref[...]
        square = res * res
        return (
            jnp.sum(fold(square * scal_ref[...]), axis=0, keepdims=True),
            jnp.sum(fold(square), axis=0, keepdims=True),
        )

    product_a, norm_a = pair(res_a, scal_a)
    product_m, norm_m = pair(res_m, scal_m)
    tile = rows_tile([product_a + marker_weight * product_m, norm_a + marker_weight * norm_m])
    out[...] = jnp.broadcast_to(tile[None], out.shape)
    token[...] = tile


def prepare_kernel(
    bits,
    genotyped,
    token,
    res,
    scal,
    direction,
    send,
    row_index,
    search_out,
    direction_out,
    search_placed,
    direction_placed,
    search_ref,
    direction_ref,
):
    del token
    traits, animals = res.shape
    base = 1 << bits
    blocks = animals // base
    search_ref[...] = jnp.zeros_like(search_ref)
    direction_ref[...] = jnp.zeros_like(direction_ref)
    search_ref[:traits] = scal[...] * res[...]
    direction_ref[:traits] = direction[...]
    table = jnp.concatenate(
        [
            parts_of(ref[:, h * base : (h + 1) * base])
            for ref in (search_ref, direction_ref)
            for h in range(blocks)
        ],
        axis=0,
    ).astype(BF16)
    size = blocks * ROWS_EACH

    def one(r):
        index = send[pl.ds(r, 1), :]
        products = dot(table, one_hot(index & (base - 1), base))
        search_out[r] = select_blocks(products[:size], index >> bits, 0, blocks)
        direction_out[r] = select_blocks(products[size:], index >> bits, 0, blocks)

    if send.shape[0] <= 8:
        for r in range(send.shape[0]):
            one(r)
    else:
        pl.loop(0, send.shape[0])(one)

    blocks = -(-genotyped // base)
    width = 1024
    total = jnp.zeros((blocks * 2 * ROWS_EACH, base), F32)
    for start in range(0, animals, width):
        window = slice(start, start + width)
        index = row_index[:, window]
        stacked = jnp.concatenate(
            [parts_of(search_ref[:, window]), parts_of(direction_ref[:, window])], axis=0
        )
        total = total + dot_t(
            masked_blocks(stacked, index >> bits, 0, blocks), one_hot(index & (base - 1), base)
        )
    for h in range(blocks):
        size = min(base, genotyped - h * base)
        for k, out in enumerate((search_placed, direction_placed)):
            start = (2 * h + k) * ROWS_EACH
            block = add_parts(total[start : start + ROWS_EACH])
            out[:, h * base : h * base + size] = block[:, :size]


def animal_kernel(sums, previous, res, scal, direction, search_out, direction_out, new_ref, out):
    traits = res.shape[0]
    conjugacy = product_of(sums) / previous[...]
    new_ref[...] = jnp.zeros_like(new_ref)
    new_ref[:traits] = scal[...] * res[...] + conjugacy * direction[...]
    out[...] = search_out[...] + conjugacy.reshape(1, 1, 1) * direction_out[...]


def chunk_copies(genotypes, buffer, semaphores):
    width = buffer.shape[2]
    return [
        pltpu.make_async_copy(
            genotypes.at[:, i * width : (i + 1) * width], buffer.at[i], semaphores.at[i]
        )
        for i in range(buffer.shape[0])
    ]


def predict_kernel(
    sums,
    previous,
    res,
    scal,
    direction,
    genotypes,
    search_placed,
    direction_placed,
    new_m,
    out,
    buffer,
    semaphores,
):
    copies = chunk_copies(genotypes, buffer, semaphores)
    for copy in copies:
        copy.start()
    traits = res.shape[0]
    conjugacy = product_of(sums) / previous[...]
    difference = search_placed[...] + conjugacy * direction_placed[...]
    new_m[...] = jnp.zeros_like(new_m)
    new_m[:traits] = scal[...] * res[...] + conjugacy * direction[...]
    width = buffer.shape[2]
    total = None
    for i, copy in enumerate(copies):
        new = new_m[:, i * width : (i + 1) * width].astype(BF16)
        copy.wait()
        term = dot_t(new, buffer[i])
        total = term if total is None else total + term
    out[...] = jnp.broadcast_to((difference - total)[None], out.shape)


def pedigree_kernel(bits, parents, new_a, sire, dam, sampling_ref, back_ref, left_ref):
    owners, _, base = parents.shape
    animals = new_a.shape[1]
    for h in range(0, owners, 2):
        left_ref[h * ROWS_EACH : (h + 2) * ROWS_EACH, :] = jnp.concatenate(
            [parts_of(parents[h]), parts_of(parents[h + 1])], axis=0
        ).astype(BF16)
    group = min(8, owners)
    groups = owners // group
    width = 1024
    slots = owners * base
    back_ref[...] = jnp.zeros_like(back_ref)
    for start in range(0, animals, width):
        window = slice(start, start + width)
        sire_index, dam_index = sire[:, window], dam[:, window]
        sire_high, dam_high = sire_index >> bits, dam_index >> bits
        sire_hot = one_hot(sire_index & (base - 1), base)
        dam_hot = one_hot(dam_index & (base - 1), base)
        gathered = jnp.zeros((PAD, width), F32)
        for g in range(groups):
            left = left_ref[g * group * ROWS_EACH : (g + 1) * group * ROWS_EACH, :]
            gathered = gathered + (
                select_blocks(dot(left, sire_hot), sire_high, g * group, group)
                + select_blocks(dot(left, dam_hot), dam_high, g * group, group)
            )
        known = (sire_index < slots).astype(F32) + (dam_index < slots).astype(F32)
        mendel = 1.0 / (1.0 - 0.25 * known)
        sampling = mendel * (new_a[:, window] - 0.5 * gathered)
        sampling_ref[:, window] = sampling
        stacked = parts_of(-0.5 * sampling)
        for g in range(groups):
            total = dot_t(masked_blocks(stacked, sire_high, g * group, group), sire_hot) + dot_t(
                masked_blocks(stacked, dam_high, g * group, group), dam_hot
            )
            for h in range(group):
                back_ref[g * group + h] += add_parts(total[h * ROWS_EACH : (h + 1) * ROWS_EACH])


def deviation_kernel(
    share,
    traits,
    differences,
    genomic,
    genotypes,
    back,
    deviation_ref,
    out,
    genomic_ref,
    buffer,
    semaphores,
):
    copies = chunk_copies(genotypes, buffer, semaphores)
    for copy in copies:
        copy.start()
    load_matrix(genomic, genomic_ref)
    deviation = apply_matrix(genomic_ref, sums_of(differences), traits)
    deviation_ref[...] = deviation
    rounded = deviation.astype(BF16)
    start = out.shape[2] - back.shape[2]
    out[:, :, start:] = back[...]
    per_chunk = buffer.shape[2] // share
    for i, copy in enumerate(copies):
        copy.wait()
        terms = dot(rounded, buffer[i])
        for j in range(per_chunk):
            pack(out, i * per_chunk + j, terms[:, j * share : (j + 1) * share], traits, share)


def record_kernel(token, sampling, new_a, pattern, table, genetic, out, matrix_ref):
    del token
    traits = genetic.shape[0]
    patterns = table.shape[1]
    load_matrix(genetic, matrix_ref)
    values = table[...]
    high = values.astype(BF16).astype(F32)
    rest = values - high
    middle = rest.astype(BF16).astype(F32)
    stacked = jnp.concatenate([high, middle, rest - middle], axis=0).astype(BF16)
    width = 1024
    size = traits * PAD
    for start in range(0, new_a.shape[1], width):
        window = slice(start, start + width)
        new = new_a[:, window]
        blocks = dot(stacked, one_hot(pattern[:, window], patterns))
        total = apply_matrix(matrix_ref, sampling[:, window], traits)
        for s in range(traits):
            row = slice(s * PAD, (s + 1) * PAD)
            block = blocks[row] + blocks[size:][row] + blocks[2 * size :][row]
            total = total + block * new[s : s + 1, :]
        out[:, window] = total


def image_kernel(
    bits,
    share,
    row,
    received,
    send,
    base_image,
    deviation,
    row_index,
    genetic,
    marker_inverse,
    new_a,
    res_a,
    new_share,
    res_share,
    image_a,
    out,
    matrix_ref,
    marker_ref,
    table_ref,
    terms_ref,
    res_ref,
):
    del row
    owners = received.shape[0]
    base = 1 << bits
    traits = genetic.shape[0]
    animals = base_image.shape[1]
    genotyped = deviation.shape[1]
    width = packed_width(traits, share)
    load_matrix(genetic, matrix_ref)
    load_matrix(marker_inverse, marker_ref)
    blocks = animals // base

    def scatter(r, total):
        index = send[pl.ds(r, 1), :]
        stacked = parts_of(received[r, :, width:])
        return total + dot_t(
            masked_blocks(stacked, index >> bits, 0, blocks), one_hot(index & (base - 1), base)
        )

    total = jnp.zeros((blocks * ROWS_EACH, base), F32)
    if owners <= 8:
        for r in range(owners):
            total = scatter(r, total)
    else:
        total = lax.fori_loop(0, owners, scatter, total)
    table_ref[...] = jnp.zeros_like(table_ref)
    table_ref[:, :genotyped] = deviation[...]
    places = table_ref.shape[1] // base
    table = jnp.concatenate(
        [parts_of(table_ref[:, h * base : (h + 1) * base]) for h in range(places)], axis=0
    ).astype(BF16)
    for h in range(blocks):
        window = slice(h * base, (h + 1) * base)
        index = row_index[:, window]
        gathered = add_parts(total[h * ROWS_EACH : (h + 1) * ROWS_EACH])
        genomic_term = select_blocks(
            dot(table, one_hot(index & (base - 1), base)), index >> bits, 0, places
        )
        image_a[:, window] = (
            base_image[:, window] + apply_matrix(matrix_ref, gathered, traits) + genomic_term
        )

    summed = received[0, :, :width]
    for i in range(1, owners):
        summed = summed + received[i, :, :width]
    terms_ref[...] = jnp.zeros_like(terms_ref)
    res_ref[...] = jnp.zeros_like(res_ref)
    res_ref[:traits, :share] = res_share[...]
    if is_packed(traits, share):
        main = share * 3 // 4
        terms_ref[:traits, :main] = summed[:traits, :main]
        for t, start, size, place, column in spare_pieces(traits, share):
            terms_ref[t : t + 1, start : start + size] = summed[
                place : place + 1, column : column + size
            ]
    else:
        terms_ref[:, :width] = summed
    new = new_share[...]
    image = apply_matrix(marker_ref, new, traits) - terms_ref[:, :share]
    terms_ref[:, :share] = image
    curvature = fold(new_a[...] * image_a[...])
    if share % LANES == 0:
        curvature = curvature + fold(new * image)
        curvature = jnp.sum(curvature, axis=0, keepdims=True)
    else:
        rest = jnp.sum(jnp.sum(new * image, axis=1, keepdims=True), axis=0, keepdims=True)
        first = lax.broadcasted_iota(jnp.int32, (1, LANES), 1) == 0
        curvature = jnp.sum(curvature, axis=0, keepdims=True) + jnp.where(first, rest, 0.0)
    tile = rows_tile(
        [curvature]
        + exact_sums(
            [
                (res_a[...], image_a[:traits]),
                (res_ref[:traits], terms_ref[:traits]),
            ]
        )
    )
    for i in range(owners):
        if not is_packed(traits, share):
            out[i] = jnp.zeros(out.shape[1:], F32)
        pack(out, i, image, traits, share)
        out[i, :, width:] = tile


def spread_kernel(received, out):
    start = received.shape[2] - LANES
    tile = exact_tile([received[i, :, start:] for i in range(received.shape[0])])
    out[...] = jnp.broadcast_to(tile[None], out.shape)


def final_kernel(
    share,
    sums,
    tiles,
    sol_a,
    res_a,
    new_a,
    image_a,
    sol_m,
    res_m,
    new_m,
    gathered,
    next_sol_a,
    next_sol_m,
    next_res_a,
    next_res_m,
    reduction,
):
    traits = sol_a.shape[0]
    tile = exact_tile([tiles[i] for i in range(tiles.shape[0])])
    step = product_of(sums) / jnp.sum(tile[0:1], axis=1, keepdims=True)
    next_sol_a[...] = sol_a[...] + step * new_a[:traits]
    next_res_a[...] = res_a[...] - step * image_a[:traits]
    next_sol_m[...] = sol_m[...] + step * new_m[:traits]
    for i in range(gathered.shape[0]):
        left = i * share
        if is_packed(traits, share):
            main = share * 3 // 4
            window = slice(left, left + main)
            next_res_m[:, window] = res_m[:, window] - step * gathered[i, :traits, :main]
            for t, start, size, place, column in spare_pieces(traits, share):
                window = slice(left + start, left + start + size)
                next_res_m[t : t + 1, window] = (
                    res_m[t : t + 1, window]
                    - step * gathered[i, place : place + 1, column : column + size]
                )
        else:
            window = slice(left, left + share)
            next_res_m[:, window] = res_m[:, window] - step * gathered[i, :traits, :share]

    step_row = jnp.broadcast_to(step, (1, LANES))
    step_halves = halves(step_row)

    def times_step(total, error):
        product, rounding = two_product(total, halves(total), step_row, step_halves)
        return product, rounding + error * step_row

    cross, cross_error = times_step(tile[3:4], tile[4:5])
    square, square_error = times_step(*times_step(tile[5:6], tile[6:7]))
    total, first = two_sum(tile[1:2], -2.0 * cross)
    total, second = two_sum(total, square)
    norm = total + (first + second + tile[2:3] - 2.0 * cross_error + square_error)
    reduction[...] = jnp.sum(norm, axis=1, keepdims=True) / norm_of(sums)


def exchange(values, axes):
    return lax.all_to_all(values, axes, split_axis=0, concat_axis=0, tiled=True)


def local(
    solution_animal,
    solution_marker,
    residual_animal,
    residual_marker,
    direction_animal,
    direction_marker,
    scaling_animal,
    scaling_marker,
    previous_product,
    genotypes,
    genetic_inverse,
    genomic_inverse,
    marker_inverse,
    residual_table,
    pattern,
    sire_slot,
    dam_slot,
    genotype_row,
    send_list,
):
    traits, animals = residual_animal.shape
    markers = residual_marker.shape[1]
    genotyped = genotypes.shape[0]
    rows = lax.axis_size("rows")
    columns = lax.axis_size("mk")
    capacity = send_list.shape[3]
    bits = capacity.bit_length() - 1
    share = markers // rows
    patterns = residual_table.shape[0]
    row = lax.axis_index("rows").astype(jnp.int32).reshape(1)
    previous = previous_product.reshape(1, 1)
    send = send_list.reshape(rows, capacity)
    sire, dam = sire_slot.reshape(1, animals), dam_slot.reshape(1, animals)
    kinds, places = pattern.reshape(1, animals), genotype_row.reshape(1, animals)
    table = jnp.pad(jnp.transpose(residual_table, (2, 1, 0)), ((0, 0), (0, PAD - traits), (0, 0)))
    table = table.reshape(traits * PAD, patterns)

    animal_block = shape_of(PAD, animals)
    slot_block = shape_of(rows, PAD, capacity)
    tile = shape_of(PAD, LANES)
    local_sums, token = call(
        functools.partial(totals_kernel, 1.0 / rows),
        (shape_of(rows * columns, PAD, LANES), tile),
        name="totals",
    )(residual_animal, scaling_animal, residual_marker, scaling_marker)
    sums = exchange(local_sums, ("rows", "mk"))
    search_out, direction_out, search_placed, direction_placed = call(
        functools.partial(prepare_kernel, bits, genotyped),
        (slot_block, slot_block, shape_of(PAD, genotyped), shape_of(PAD, genotyped)),
        (pltpu.VMEM((PAD, animals), F32), pltpu.VMEM((PAD, animals), F32)),
        name="prepare",
    )(token, residual_animal, scaling_animal, direction_animal, send, places)
    sums, table = lax.optimization_barrier((sums, table))
    new_animal, outgoing = call(animal_kernel, (animal_block, slot_block), name="animals")(
        sums,
        previous,
        residual_animal,
        scaling_animal,
        direction_animal,
        search_out,
        direction_out,
    )
    parents = exchange(outgoing, "rows")

    def whole(count):
        return [pl.BlockSpec(memory_space=pltpu.VMEM)] * count

    off_chip = [pl.BlockSpec(memory_space=pl.ANY)]
    chunk = 2 * share * max(1, 1536 // share)
    new_marker, difference = call(
        predict_kernel,
        (shape_of(PAD, markers), shape_of(columns, PAD, genotyped)),
        (
            pltpu.VMEM((markers // chunk, genotyped, chunk), BF16),
            pltpu.SemaphoreType.DMA((markers // chunk,)),
        ),
        in_specs=whole(5) + off_chip + whole(2),
        name="predict",
    )(
        sums,
        previous,
        residual_marker,
        scaling_marker,
        direction_marker,
        genotypes,
        search_placed,
        direction_placed,
    )
    differences = exchange(difference, "mk")
    sampling, back = call(
        functools.partial(pedigree_kernel, bits),
        (animal_block, slot_block),
        (pltpu.VMEM((rows * ROWS_EACH, capacity), BF16),),
        name="pedigree",
    )(parents, new_animal, sire, dam)
    chunk = share * max(1, 1536 // share)
    width = packed_width(traits, share)
    deviation, payload = call(
        functools.partial(deviation_kernel, share, traits),
        (shape_of(PAD, genotyped), shape_of(rows, PAD, width + capacity)),
        (
            pltpu.VMEM((PAD, LANES), F32),
            pltpu.VMEM((markers // chunk, genotyped, chunk), BF16),
            pltpu.SemaphoreType.DMA((markers // chunk,)),
        ),
        in_specs=whole(2) + off_chip + whole(1),
        name="deviation",
    )(differences, genomic_inverse, genotypes, back)
    received = exchange(payload, "rows")
    base_image = call(record_kernel, animal_block, (pltpu.VMEM((PAD, LANES), F32),), name="record")(
        deviation, sampling, new_animal, kinds, table, genetic_inverse
    )

    if share % LANES:
        start = row[0] * share
        new_share = lax.dynamic_slice_in_dim(new_marker, start, share, 1)
        res_share = lax.dynamic_slice_in_dim(residual_marker, start, share, 1)

        def own(height):
            return pl.BlockSpec((height, share), lambda k, r: (0, 0))
    else:
        new_share, res_share = new_marker, residual_marker

        def own(height):
            return pl.BlockSpec((height, share), lambda k, r: (0, r[0]))

    def still(array):
        return pl.BlockSpec(array.shape, lambda k, r, n=len(array.shape): (0,) * n)

    out_shape = shape_of(rows, PAD, width + LANES)
    full = -(-share // LANES) * LANES
    inputs = (
        received,
        send,
        base_image,
        deviation,
        places,
        genetic_inverse,
        marker_inverse,
        new_animal,
        residual_animal,
    )
    image_animal, payload = pl.pallas_call(
        functools.partial(image_kernel, bits, share),
        out_shape=(animal_block, out_shape),
        grid_spec=pltpu.PrefetchScalarGridSpec(
            num_scalar_prefetch=1,
            grid=(1,),
            in_specs=[still(array) for array in inputs] + [own(PAD), own(traits)],
            out_specs=(still(animal_block), still(out_shape)),
            scratch_shapes=[
                pltpu.VMEM((PAD, LANES), F32),
                pltpu.VMEM((PAD, LANES), F32),
                pltpu.VMEM((PAD, -(-genotyped // capacity) * capacity), F32),
                pltpu.VMEM((PAD, full), F32),
                pltpu.VMEM((PAD, full), F32),
            ],
        ),
        name="image",
    )(row, *inputs, new_share, res_share)
    gathered = exchange(payload, "rows")
    tiles = exchange(
        call(spread_kernel, shape_of(columns, PAD, LANES), name="spread")(gathered), "mk"
    )
    *outputs, reduction = call(
        functools.partial(final_kernel, share),
        (
            shape_of(traits, animals),
            shape_of(traits, markers),
            shape_of(traits, animals),
            shape_of(traits, markers),
            shape_of(1, 1),
        ),
        name="final",
    )(
        sums,
        tiles,
        solution_animal,
        residual_animal,
        new_animal,
        image_animal,
        solution_marker,
        residual_marker,
        new_marker,
        gathered,
    )
    return (*outputs, reduction.reshape(()))


def solution(mesh):
    animal, marker = P(None, ("rows", "mk")), P(None, "mk")
    index = P(("rows", "mk"))
    return jax.shard_map(
        local,
        mesh=mesh,
        in_specs=(
            animal,
            marker,
            animal,
            marker,
            animal,
            marker,
            animal,
            marker,
            P(),
            P("rows", "mk"),
            P(),
            P(),
            P(),
            P(),
            index,
            index,
            index,
            index,
            P("rows", "mk", None, None),
        ),
        out_specs=(animal, marker, animal, marker, P()),
        check_vma=False,
    )
```

```python
import functools

import jax
import jax.numpy as jnp
from jax import lax
from jax.experimental import pallas as pl
from jax.experimental.pallas import tpu as pltpu
from jax.sharding import PartitionSpec as P

F32 = jnp.float32
BF16 = jnp.bfloat16
PAD = 8
LANES = 128


def shape_of(*dims, dtype=F32):
    return jax.ShapeDtypeStruct(dims, dtype)


LIMIT = pltpu.CompilerParams(vmem_limit_bytes=24 << 20)


def call(kernel, out_shape, scratch=(), **options):
    return pl.pallas_call(
        kernel,
        out_shape=out_shape,
        scratch_shapes=list(scratch),
        compiler_params=LIMIT,
        **options,
    )


def parts_of(values):
    high = values.astype(BF16).astype(F32)
    rest = values - high
    middle = rest.astype(BF16).astype(F32)
    return jnp.concatenate([high, middle, rest - middle], axis=0)


def add_parts(stacked):
    return stacked[:PAD] + stacked[PAD : 2 * PAD] + stacked[2 * PAD :]


ROWS_EACH = 3 * PAD


def one_hot(low, base):
    wanted = lax.broadcasted_iota(jnp.int32, (base, low.shape[1]), 0)
    return jnp.where(wanted == low, 1.0, 0.0).astype(BF16)


def dot(left, right):
    return lax.dot_general(left, right, (((1,), (0,)), ((), ())), preferred_element_type=F32)


def dot_t(left, right):
    return lax.dot_general(left, right, (((1,), (1,)), ((), ())), preferred_element_type=F32)


def select_blocks(products, high, first, count):
    total = None
    for h in range(count):
        block = add_parts(products[h * ROWS_EACH : (h + 1) * ROWS_EACH])
        block = jnp.where(high == first + h, block, 0.0)
        total = block if total is None else total + block
    return total


def masked_blocks(stacked, high, first, count):
    return jnp.concatenate(
        [jnp.where(high == first + h, stacked, 0.0) for h in range(count)], axis=0
    ).astype(BF16)


def fold(values):
    total = values[:, :LANES]
    for start in range(LANES, values.shape[1], LANES):
        total = total + values[:, start : start + LANES]
    return total


def load_matrix(matrix_ref, padded_ref):
    padded_ref[...] = jnp.zeros_like(padded_ref)
    size = matrix_ref.shape[0]
    padded_ref[:size, :size] = matrix_ref[...]


def apply_matrix(padded_ref, values, count):
    total = None
    for s in range(count):
        term = padded_ref[:, s : s + 1] * values[s : s + 1, :]
        total = term if total is None else total + term
    return total


def sums_of(received_ref):
    tile = received_ref[0]
    for i in range(1, received_ref.shape[0]):
        tile = tile + received_ref[i]
    return tile


def product_of(sums_ref):
    return jnp.sum(sums_of(sums_ref)[0:1], axis=1, keepdims=True)


def norm_of(sums_ref):
    return jnp.sum(sums_of(sums_ref)[1:2], axis=1, keepdims=True)


def two_sum(left, right):
    total = left + right
    back = total - left
    return total, (left - (total - back)) + (right - back)


def halves(values):
    scaled = values * 4097.0
    high = scaled - (scaled - values)
    return high, values - high


def two_product(left, left_halves, right, right_halves):
    product = left * right
    (lh, ll), (rh, rl) = left_halves, right_halves
    return product, ((lh * rh - product) + lh * rl + ll * rh) + ll * rl


def exact_sums(pairs):
    columns = []
    for left, right in pairs:
        lh, rh = halves(left), halves(right)
        for a, ah, b, bh in ((left, lh, left, lh), (left, lh, right, rh), (right, rh, right, rh)):
            columns.append(two_product(a, ah, b, bh))
    results = []
    for kind in range(3):
        total = error = None
        for product, rounding in columns[kind::3]:
            for start in range(0, product.shape[1], LANES):
                window = slice(start, start + LANES)
                if total is None:
                    total, error = product[:, window], rounding[:, window]
                else:
                    total, extra = two_sum(total, product[:, window])
                    error = error + (extra + rounding[:, window])
        row, rest = total[0:1], error[0:1]
        for t in range(1, total.shape[0]):
            row, extra = two_sum(row, total[t : t + 1])
            rest = rest + (extra + error[t : t + 1])
        results += [row, rest]
    return results


def rows_tile(rows):
    place = lax.broadcasted_iota(jnp.int32, (PAD, LANES), 0)
    tile = jnp.zeros((PAD, LANES), F32)
    for k, row in enumerate(rows):
        tile = jnp.where(place == k, row, tile)
    return tile


def exact_tile(tiles):
    total = tiles[0]
    error = jnp.zeros_like(total)
    for tile in tiles[1:]:
        total, extra = two_sum(total, tile)
        error = error + extra
    place = lax.broadcasted_iota(jnp.int32, (PAD, LANES), 0)
    errors = (place == 2) | (place == 4) | (place == 6)
    return total + jnp.where(errors, pltpu.roll(error, 1, 0), 0.0)


def is_packed(traits, share):
    return traits == 6 and share % (4 * LANES) == 0


def packed_width(traits, share):
    return share * 3 // 4 if is_packed(traits, share) else -(-share // LANES) * LANES


def spare_pieces(traits, share):
    main, rest = share * 3 // 4, share // 4
    return [
        (t, main, rest, traits + t // 3, t % 3 * rest)
        for t in range(traits if is_packed(traits, share) else 0)
    ]


def pack(out, i, values, traits, share):
    if not is_packed(traits, share):
        out[i, :, :share] = values
        return
    main = share * 3 // 4
    out[i, :traits, :main] = values[:traits, :main]
    for t, start, width, row, column in spare_pieces(traits, share):
        out[i, row : row + 1, column : column + width] = values[t : t + 1, start : start + width]


def totals_kernel(marker_weight, res_a, scal_a, res_m, scal_m, out, token):
    def pair(res_ref, scal_ref):
        res = res_ref[...]
        square = res * res
        return (
            jnp.sum(fold(square * scal_ref[...]), axis=0, keepdims=True),
            jnp.sum(fold(square), axis=0, keepdims=True),
        )

    product_a, norm_a = pair(res_a, scal_a)
    product_m, norm_m = pair(res_m, scal_m)
    tile = rows_tile([product_a + marker_weight * product_m, norm_a + marker_weight * norm_m])
    out[...] = jnp.broadcast_to(tile[None], out.shape)
    token[...] = tile


def prepare_kernel(
    bits,
    genotyped,
    token,
    res,
    scal,
    direction,
    send,
    row_index,
    res_m,
    scal_m,
    direction_m,
    search_out,
    direction_out,
    search_placed,
    direction_placed,
    search_ref,
    direction_ref,
    search_m,
    direction_m8,
):
    del token
    traits, animals = res.shape
    base = 1 << bits
    blocks = animals // base
    search_ref[...] = jnp.zeros_like(search_ref)
    direction_ref[...] = jnp.zeros_like(direction_ref)
    search_ref[:traits] = scal[...] * res[...]
    direction_ref[:traits] = direction[...]
    table = jnp.concatenate(
        [
            parts_of(ref[:, h * base : (h + 1) * base])
            for ref in (search_ref, direction_ref)
            for h in range(blocks)
        ],
        axis=0,
    ).astype(BF16)
    size = blocks * ROWS_EACH

    def one(r):
        index = send[pl.ds(r, 1), :]
        products = dot(table, one_hot(index & (base - 1), base))
        search_out[r] = select_blocks(products[:size], index >> bits, 0, blocks)
        direction_out[r] = select_blocks(products[size:], index >> bits, 0, blocks)

    if send.shape[0] <= 8:
        for r in range(send.shape[0]):
            one(r)
    else:
        pl.loop(0, send.shape[0])(one)

    blocks = -(-genotyped // base)
    width = 1024
    total = jnp.zeros((blocks * 2 * ROWS_EACH, base), F32)
    for start in range(0, animals, width):
        window = slice(start, start + width)
        index = row_index[:, window]
        stacked = jnp.concatenate(
            [parts_of(search_ref[:, window]), parts_of(direction_ref[:, window])], axis=0
        )
        total = total + dot_t(
            masked_blocks(stacked, index >> bits, 0, blocks), one_hot(index & (base - 1), base)
        )
    for h in range(blocks):
        size = min(base, genotyped - h * base)
        for k, out in enumerate((search_placed, direction_placed)):
            start = (2 * h + k) * ROWS_EACH
            block = add_parts(total[start : start + ROWS_EACH])
            out[:, h * base : h * base + size] = block[:, :size]
    search_m[...] = jnp.zeros_like(search_m)
    direction_m8[...] = jnp.zeros_like(direction_m8)
    search_m[:traits] = scal_m[...] * res_m[...]
    direction_m8[:traits] = direction_m[...]


def animal_kernel(sums, previous, search, direction, search_out, direction_out, new_ref, out):
    conjugacy = product_of(sums) / previous[...]
    new_ref[...] = search[...] + conjugacy * direction[...]
    out[...] = search_out[...] + conjugacy.reshape(1, 1, 1) * direction_out[...]


def chunk_copies(genotypes, buffer, semaphores):
    width = buffer.shape[2]
    copies = [
        pltpu.make_async_copy(
            genotypes.at[:, i * width : (i + 1) * width], buffer.at[i], semaphores.at[i]
        )
        for i in range(buffer.shape[0])
    ]
    for copy in copies:
        copy.start()
    return copies


def predict_kernel(
    sums,
    previous,
    search,
    direction,
    genotypes,
    search_placed,
    direction_placed,
    new_m,
    out,
    buffer,
    semaphores,
):
    copies = chunk_copies(genotypes, buffer, semaphores)
    conjugacy = product_of(sums) / previous[...]
    new_m[...] = search[...] + conjugacy * direction[...]
    total = search_placed[...] + conjugacy * direction_placed[...]
    width = buffer.shape[2]
    for i, copy in enumerate(copies):
        new = new_m[:, i * width : (i + 1) * width].astype(BF16)
        copy.wait()
        total = total - dot_t(new, buffer[i])
    out[...] = total


def pedigree_kernel(bits, parents, new_a, sire, dam, sampling_ref, back_ref, left_ref):
    owners, _, base = parents.shape
    animals = new_a.shape[1]
    for h in range(0, owners, 2):
        left_ref[h * ROWS_EACH : (h + 2) * ROWS_EACH, :] = jnp.concatenate(
            [parts_of(parents[h]), parts_of(parents[h + 1])], axis=0
        ).astype(BF16)
    group = min(8, owners)
    groups = owners // group
    width = 1024
    slots = owners * base
    back_ref[...] = jnp.zeros_like(back_ref)
    for start in range(0, animals, width):
        window = slice(start, start + width)
        sire_index, dam_index = sire[:, window], dam[:, window]
        sire_high, dam_high = sire_index >> bits, dam_index >> bits
        sire_hot = one_hot(sire_index & (base - 1), base)
        dam_hot = one_hot(dam_index & (base - 1), base)
        gathered = jnp.zeros((PAD, width), F32)
        for g in range(groups):
            left = left_ref[g * group * ROWS_EACH : (g + 1) * group * ROWS_EACH, :]
            gathered = gathered + (
                select_blocks(dot(left, sire_hot), sire_high, g * group, group)
                + select_blocks(dot(left, dam_hot), dam_high, g * group, group)
            )
        known = (sire_index < slots).astype(F32) + (dam_index < slots).astype(F32)
        mendel = 1.0 / (1.0 - 0.25 * known)
        sampling = mendel * (new_a[:, window] - 0.5 * gathered)
        sampling_ref[:, window] = sampling
        stacked = parts_of(-0.5 * sampling)
        for g in range(groups):
            total = dot_t(masked_blocks(stacked, sire_high, g * group, group), sire_hot) + dot_t(
                masked_blocks(stacked, dam_high, g * group, group), dam_hot
            )
            for h in range(group):
                back_ref[g * group + h] += add_parts(total[h * ROWS_EACH : (h + 1) * ROWS_EACH])


def deviation_kernel(share, traits, columns, *refs):
    deviation_body(share, traits, refs[:columns], *refs[columns:])


def deviation_body(
    share,
    traits,
    differences,
    genomic,
    genotypes,
    back,
    deviation_ref,
    out,
    genomic_ref,
    buffer,
    semaphores,
):
    copies = chunk_copies(genotypes, buffer, semaphores)
    load_matrix(genomic, genomic_ref)
    difference = differences[0][...]
    for other in differences[1:]:
        difference = difference + other[...]
    deviation = apply_matrix(genomic_ref, difference, traits)
    deviation_ref[...] = deviation
    rounded = deviation.astype(BF16)
    start = out.shape[2] - back.shape[2]
    out[:, :, start:] = back[...]
    per_chunk = buffer.shape[2] // share
    for i, copy in enumerate(copies):
        copy.wait()
        terms = dot(rounded, buffer[i])
        for j in range(per_chunk):
            pack(out, i * per_chunk + j, terms[:, j * share : (j + 1) * share], traits, share)


def record_kernel(token, sampling, new_a, pattern, table, genetic, out, matrix_ref):
    del token
    traits = genetic.shape[0]
    patterns = table.shape[1]
    load_matrix(genetic, matrix_ref)
    values = table[...]
    high = values.astype(BF16).astype(F32)
    rest = values - high
    middle = rest.astype(BF16).astype(F32)
    stacked = jnp.concatenate([high, middle, rest - middle], axis=0).astype(BF16)
    width = 1024
    size = traits * PAD
    for start in range(0, new_a.shape[1], width):
        window = slice(start, start + width)
        new = new_a[:, window]
        blocks = dot(stacked, one_hot(pattern[:, window], patterns))
        total = apply_matrix(matrix_ref, sampling[:, window], traits)
        for s in range(traits):
            row = slice(s * PAD, (s + 1) * PAD)
            block = blocks[row] + blocks[size:][row] + blocks[2 * size :][row]
            total = total + block * new[s : s + 1, :]
        out[:, window] = total


def image_kernel(
    bits,
    share,
    row,
    received,
    send,
    base_image,
    deviation,
    row_index,
    genetic,
    marker_inverse,
    new_a,
    res_a,
    new_share,
    res_share,
    image_a,
    out,
    matrix_ref,
    marker_ref,
    table_ref,
    terms_ref,
    res_ref,
):
    del row
    owners = received.shape[0]
    base = 1 << bits
    traits = genetic.shape[0]
    animals = base_image.shape[1]
    genotyped = deviation.shape[1]
    width = packed_width(traits, share)
    load_matrix(genetic, matrix_ref)
    load_matrix(marker_inverse, marker_ref)
    blocks = animals // base

    def scatter(r, total):
        index = send[pl.ds(r, 1), :]
        stacked = parts_of(received[r, :, width:])
        return total + dot_t(
            masked_blocks(stacked, index >> bits, 0, blocks), one_hot(index & (base - 1), base)
        )

    total = jnp.zeros((blocks * ROWS_EACH, base), F32)
    if owners <= 8:
        for r in range(owners):
            total = scatter(r, total)
    else:
        total = lax.fori_loop(0, owners, scatter, total)
    table_ref[...] = jnp.zeros_like(table_ref)
    table_ref[:, :genotyped] = deviation[...]
    places = table_ref.shape[1] // base
    table = jnp.concatenate(
        [parts_of(table_ref[:, h * base : (h + 1) * base]) for h in range(places)], axis=0
    ).astype(BF16)
    for h in range(blocks):
        window = slice(h * base, (h + 1) * base)
        index = row_index[:, window]
        gathered = add_parts(total[h * ROWS_EACH : (h + 1) * ROWS_EACH])
        genomic_term = select_blocks(
            dot(table, one_hot(index & (base - 1), base)), index >> bits, 0, places
        )
        image_a[:, window] = (
            base_image[:, window] + apply_matrix(matrix_ref, gathered, traits) + genomic_term
        )

    summed = received[0, :, :width]
    for i in range(1, owners):
        summed = summed + received[i, :, :width]
    terms_ref[...] = jnp.zeros_like(terms_ref)
    res_ref[...] = jnp.zeros_like(res_ref)
    res_ref[:traits, :share] = res_share[...]
    if is_packed(traits, share):
        main = share * 3 // 4
        terms_ref[:traits, :main] = summed[:traits, :main]
        for t, start, size, place, column in spare_pieces(traits, share):
            terms_ref[t : t + 1, start : start + size] = summed[
                place : place + 1, column : column + size
            ]
    else:
        terms_ref[:, :width] = summed
    new = new_share[...]
    image = apply_matrix(marker_ref, new, traits) - terms_ref[:, :share]
    terms_ref[:, :share] = image
    curvature = fold(new_a[...] * image_a[...])
    if share % LANES == 0:
        curvature = curvature + fold(new * image)
        curvature = jnp.sum(curvature, axis=0, keepdims=True)
    else:
        rest = jnp.sum(jnp.sum(new * image, axis=1, keepdims=True), axis=0, keepdims=True)
        first = lax.broadcasted_iota(jnp.int32, (1, LANES), 1) == 0
        curvature = jnp.sum(curvature, axis=0, keepdims=True) + jnp.where(first, rest, 0.0)
    tile = rows_tile(
        [curvature]
        + exact_sums(
            [
                (res_a[...], image_a[:traits]),
                (res_ref[:traits], terms_ref[:traits]),
            ]
        )
    )
    for i in range(owners):
        if not is_packed(traits, share):
            out[i] = jnp.zeros(out.shape[1:], F32)
        pack(out, i, image, traits, share)
        out[i, :, width:] = tile


def spread_kernel(received, out):
    start = received.shape[2] - LANES
    tile = exact_tile([received[i, :, start:] for i in range(received.shape[0])])
    out[...] = tile


def final_kernel(
    share,
    columns,
    sums,
    *refs,
):
    tiles = refs[:columns]
    final_body(share, sums, tiles, *refs[columns:])


def final_body(
    share,
    sums,
    tiles,
    sol_a,
    res_a,
    new_a,
    image_a,
    sol_m,
    res_m,
    new_m,
    gathered,
    next_sol_a,
    next_sol_m,
    next_res_a,
    next_res_m,
    reduction,
):
    traits = sol_a.shape[0]
    tile = exact_tile([ref[...] for ref in tiles])
    step = product_of(sums) / jnp.sum(tile[0:1], axis=1, keepdims=True)
    next_sol_a[...] = sol_a[...] + step * new_a[:traits]
    next_res_a[...] = res_a[...] - step * image_a[:traits]
    next_sol_m[...] = sol_m[...] + step * new_m[:traits]
    for i in range(gathered.shape[0]):
        left = i * share
        if is_packed(traits, share):
            main = share * 3 // 4
            window = slice(left, left + main)
            next_res_m[:, window] = res_m[:, window] - step * gathered[i, :traits, :main]
            for t, start, size, place, column in spare_pieces(traits, share):
                window = slice(left + start, left + start + size)
                next_res_m[t : t + 1, window] = (
                    res_m[t : t + 1, window]
                    - step * gathered[i, place : place + 1, column : column + size]
                )
        else:
            window = slice(left, left + share)
            next_res_m[:, window] = res_m[:, window] - step * gathered[i, :traits, :share]

    step_row = jnp.broadcast_to(step, (1, LANES))
    step_halves = halves(step_row)

    def times_step(total, error):
        product, rounding = two_product(total, halves(total), step_row, step_halves)
        return product, rounding + error * step_row

    cross, cross_error = times_step(tile[3:4], tile[4:5])
    square, square_error = times_step(*times_step(tile[5:6], tile[6:7]))
    total, first = two_sum(tile[1:2], -2.0 * cross)
    total, second = two_sum(total, square)
    norm = total + (first + second + tile[2:3] - 2.0 * cross_error + square_error)
    reduction[...] = jnp.sum(norm, axis=1, keepdims=True) / norm_of(sums)


def exchange(values, axes):
    return lax.all_to_all(values, axes, split_axis=0, concat_axis=0, tiled=True)


def copies_of(values, axis):
    size = lax.axis_size(axis)
    return [values] + [
        lax.ppermute(values, axis, [(i, (i + k) % size) for i in range(size)])
        for k in range(1, size)
    ]


def local(
    solution_animal,
    solution_marker,
    residual_animal,
    residual_marker,
    direction_animal,
    direction_marker,
    scaling_animal,
    scaling_marker,
    previous_product,
    genotypes,
    genetic_inverse,
    genomic_inverse,
    marker_inverse,
    residual_table,
    pattern,
    sire_slot,
    dam_slot,
    genotype_row,
    send_list,
):
    traits, animals = residual_animal.shape
    markers = residual_marker.shape[1]
    genotyped = genotypes.shape[0]
    rows = lax.axis_size("rows")
    columns = lax.axis_size("mk")
    capacity = send_list.shape[3]
    bits = capacity.bit_length() - 1
    share = markers // rows
    patterns = residual_table.shape[0]
    row = lax.axis_index("rows").astype(jnp.int32).reshape(1)
    previous = previous_product.reshape(1, 1)
    send = send_list.reshape(rows, capacity)
    sire, dam = sire_slot.reshape(1, animals), dam_slot.reshape(1, animals)
    kinds, places = pattern.reshape(1, animals), genotype_row.reshape(1, animals)
    def hbm(*arrays):
        return [pltpu.with_memory_space_constraint(array, pltpu.HBM) for array in arrays]

    animal_block = shape_of(PAD, animals)
    slot_block = shape_of(rows, PAD, capacity)
    tile = shape_of(PAD, LANES)
    local_sums, token = call(
        functools.partial(totals_kernel, 1.0 / rows),
        (shape_of(rows * columns, PAD, LANES), tile),
        name="totals",
    )(*hbm(residual_animal, scaling_animal, residual_marker, scaling_marker))
    sums = exchange(local_sums, ("rows", "mk"))
    in_vmem, in_hbm = pl.BlockSpec(memory_space=pltpu.VMEM), pl.BlockSpec(memory_space=pl.ANY)

    placed_block, marker_block = shape_of(PAD, genotyped), shape_of(PAD, markers)
    (
        search_out,
        direction_out,
        search_placed,
        direction_placed,
        search_animal,
        padded_direction,
        search_marker,
        padded_marker,
    ) = call(
        functools.partial(prepare_kernel, bits, genotyped),
        (slot_block, slot_block, placed_block, placed_block)
        + (animal_block, animal_block, marker_block, marker_block),
        name="prepare",
    )(
        token,
        *hbm(residual_animal, scaling_animal, direction_animal, send, places),
        *hbm(residual_marker, scaling_marker, direction_marker),
    )
    new_animal, outgoing = call(animal_kernel, (animal_block, slot_block), name="animals")(
        sums, previous, search_animal, padded_direction, search_out, direction_out
    )
    parents = exchange(outgoing, "rows")

    (genotypes,) = hbm(genotypes)

    def chunks(width):
        return (
            pltpu.VMEM((markers // width, genotyped, width), BF16),
            pltpu.SemaphoreType.DMA((markers // width,)),
        )

    chunk = share * max(1, 1536 // share)
    new_marker, difference = call(
        predict_kernel,
        (marker_block, placed_block),
        chunks(2 * chunk),
        in_specs=[in_vmem] * 4 + [in_hbm] + [in_vmem] * 2,
        name="predict",
    )(
        sums,
        previous,
        search_marker,
        padded_marker,
        genotypes,
        search_placed,
        direction_placed,
    )
    differences = copies_of(difference, "mk")
    sampling, back = call(
        functools.partial(pedigree_kernel, bits),
        (animal_block, slot_block),
        (pltpu.VMEM((rows * ROWS_EACH, capacity), BF16),),
        name="pedigree",
    )(parents, new_animal, sire, dam)
    width = packed_width(traits, share)
    deviation, payload = call(
        functools.partial(deviation_kernel, share, traits, columns),
        (placed_block, shape_of(rows, PAD, width + capacity)),
        (pltpu.VMEM((PAD, LANES), F32), *chunks(chunk)),
        in_specs=[in_vmem] * (columns + 1) + [in_hbm, in_vmem],
        name="deviation",
    )(*differences, genomic_inverse, genotypes, back)
    received = exchange(payload, "rows")
    residual_table, deviation = lax.optimization_barrier((residual_table, deviation))
    table = jnp.pad(jnp.transpose(residual_table, (2, 1, 0)), ((0, 0), (0, PAD - traits), (0, 0)))
    table = table.reshape(traits * PAD, patterns)
    base_image = call(record_kernel, animal_block, (pltpu.VMEM((PAD, LANES), F32),), name="record")(
        deviation, sampling, new_animal, kinds, table, genetic_inverse
    )

    if share % LANES:
        start = row[0] * share
        new_share = lax.dynamic_slice_in_dim(new_marker, start, share, 1)
        res_share = lax.dynamic_slice_in_dim(residual_marker, start, share, 1)

        def own(height):
            return pl.BlockSpec((height, share), lambda k, r: (0, 0))
    else:
        new_share, res_share = new_marker, residual_marker

        def own(height):
            return pl.BlockSpec((height, share), lambda k, r: (0, r[0]))

    def still(array):
        return pl.BlockSpec(array.shape, lambda k, r, n=len(array.shape): (0,) * n)

    out_shape = shape_of(rows, PAD, width + LANES)
    full = -(-share // LANES) * LANES
    inputs = (
        received,
        send,
        base_image,
        deviation,
        places,
        genetic_inverse,
        marker_inverse,
        new_animal,
        residual_animal,
    )
    image_animal, payload = pl.pallas_call(
        functools.partial(image_kernel, bits, share),
        out_shape=(animal_block, out_shape),
        grid_spec=pltpu.PrefetchScalarGridSpec(
            num_scalar_prefetch=1,
            grid=(1,),
            in_specs=[still(array) for array in inputs] + [own(PAD), own(traits)],
            out_specs=(still(animal_block), still(out_shape)),
            scratch_shapes=[
                pltpu.VMEM((PAD, LANES), F32),
                pltpu.VMEM((PAD, LANES), F32),
                pltpu.VMEM((PAD, -(-genotyped // capacity) * capacity), F32),
                pltpu.VMEM((PAD, full), F32),
                pltpu.VMEM((PAD, full), F32),
            ],
        ),
        compiler_params=LIMIT,
        name="image",
    )(row, *inputs, new_share, res_share)
    gathered = exchange(payload, "rows")
    tiles = copies_of(call(spread_kernel, tile, name="spread")(gathered), "mk")
    *outputs, reduction = call(
        functools.partial(final_kernel, share, columns),
        (
            shape_of(traits, animals),
            shape_of(traits, markers),
            shape_of(traits, animals),
            shape_of(traits, markers),
            shape_of(1, 1),
        ),
        name="final",
    )(
        sums,
        *tiles,
        solution_animal,
        residual_animal,
        new_animal,
        image_animal,
        solution_marker,
        residual_marker,
        new_marker,
        gathered,
    )
    return (*outputs, reduction.reshape(()))


def solution(mesh):
    animal, marker = P(None, ("rows", "mk")), P(None, "mk")
    index = P(("rows", "mk"))
    return jax.shard_map(
        local,
        mesh=mesh,
        in_specs=(
            animal,
            marker,
            animal,
            marker,
            animal,
            marker,
            animal,
            marker,
            P(),
            P("rows", "mk"),
            P(),
            P(),
            P(),
            P(),
            index,
            index,
            index,
            index,
            P("rows", "mk", None, None),
        ),
        out_specs=(animal, marker, animal, marker, P()),
        check_vma=False,
    )
```

```python
import functools

import jax
import jax.numpy as jnp
from jax import lax
from jax.experimental import pallas as pl
from jax.experimental.pallas import tpu as pltpu
from jax.sharding import PartitionSpec as P

F32 = jnp.float32
BF16 = jnp.bfloat16
PAD = 8
LANES = 128


def shape_of(*dims, dtype=F32):
    return jax.ShapeDtypeStruct(dims, dtype)


LIMIT = pltpu.CompilerParams(vmem_limit_bytes=24 << 20)


def call(kernel, out_shape, scratch=(), **options):
    return pl.pallas_call(
        kernel,
        out_shape=out_shape,
        scratch_shapes=list(scratch),
        compiler_params=LIMIT,
        **options,
    )


def parts_of(values):
    high = values.astype(BF16).astype(F32)
    rest = values - high
    middle = rest.astype(BF16).astype(F32)
    return jnp.concatenate([high, middle, rest - middle], axis=0)


def add_parts(stacked):
    return stacked[:PAD] + stacked[PAD : 2 * PAD] + stacked[2 * PAD :]


ROWS_EACH = 3 * PAD


def one_hot(low, base):
    wanted = lax.broadcasted_iota(jnp.int32, (base, LANES), 0).astype(F32).astype(BF16)
    wanted = jnp.concatenate([wanted] * (low.shape[1] // LANES), axis=1)
    found = wanted == low.astype(F32).astype(BF16)
    return jnp.where(found, jnp.ones((), BF16), jnp.zeros((), BF16))


def dot(left, right):
    return lax.dot_general(left, right, (((1,), (0,)), ((), ())), preferred_element_type=F32)


def dot_t(left, right):
    return lax.dot_general(left, right, (((1,), (1,)), ((), ())), preferred_element_type=F32)


def select_blocks(products, high, first, count):
    total = None
    for h in range(count):
        block = add_parts(products[h * ROWS_EACH : (h + 1) * ROWS_EACH])
        block = jnp.where(high == first + h, block, 0.0)
        total = block if total is None else total + block
    return total


def doubled_parts(values):
    stacked = parts_of(values)
    parts = [stacked[p * PAD : (p + 1) * PAD] for p in range(3)]
    return [jnp.concatenate([part, part], axis=0).astype(BF16) for part in parts]


def masked_blocks(parts, high, first, count):
    half = lax.broadcasted_iota(jnp.int32, (2 * PAD, LANES), 0) // PAD
    half = half.astype(F32).astype(BF16)
    half = jnp.concatenate([half] * (high.shape[1] // LANES), axis=1)
    tiles = []
    for pair in range(0, count, 2):
        found = half == (high - (first + pair)).astype(F32).astype(BF16)
        tiles += [jnp.where(found, part, jnp.zeros((), BF16)) for part in parts]
    return jnp.concatenate(tiles, axis=0)


def block_of(total, h, kinds=1, kind=0):
    start = (h // 2 * kinds + kind) * 3 * 2 * PAD + h % 2 * PAD
    rows = [total[start + p * 2 * PAD : start + p * 2 * PAD + PAD] for p in range(3)]
    return rows[0] + rows[1] + rows[2]


def fold(values):
    total = values[:, :LANES]
    for start in range(LANES, values.shape[1], LANES):
        total = total + values[:, start : start + LANES]
    return total


def load_matrix(matrix_ref, padded_ref):
    padded_ref[...] = jnp.zeros_like(padded_ref)
    size = matrix_ref.shape[0]
    padded_ref[:size, :size] = matrix_ref[...]


def apply_matrix(padded_ref, values, count):
    total = None
    for s in range(count):
        term = padded_ref[:, s : s + 1] * values[s : s + 1, :]
        total = term if total is None else total + term
    return total


def sums_of(received_ref):
    tile = received_ref[0]
    for i in range(1, received_ref.shape[0]):
        tile = tile + received_ref[i]
    return tile


def product_of(sums_ref):
    return jnp.sum(sums_of(sums_ref)[0:1], axis=1, keepdims=True)


def norm_of(sums_ref):
    return jnp.sum(sums_of(sums_ref)[1:2], axis=1, keepdims=True)


def two_sum(left, right):
    total = left + right
    back = total - left
    return total, (left - (total - back)) + (right - back)


def halves(values):
    scaled = values * 4097.0
    high = scaled - (scaled - values)
    return high, values - high


def two_product(left, left_halves, right, right_halves):
    product = left * right
    (lh, ll), (rh, rl) = left_halves, right_halves
    return product, ((lh * rh - product) + lh * rl + ll * rh) + ll * rl


def exact_sums(pairs):
    columns = []
    for left, right in pairs:
        lh, rh = halves(left), halves(right)
        for a, ah, b, bh in ((left, lh, left, lh), (left, lh, right, rh), (right, rh, right, rh)):
            columns.append(two_product(a, ah, b, bh))
    results = []
    for kind in range(3):
        total = error = None
        for product, rounding in columns[kind::3]:
            for start in range(0, product.shape[1], LANES):
                window = slice(start, start + LANES)
                if total is None:
                    total, error = product[:, window], rounding[:, window]
                else:
                    total, extra = two_sum(total, product[:, window])
                    error = error + (extra + rounding[:, window])
        row, rest = total[0:1], error[0:1]
        for t in range(1, total.shape[0]):
            row, extra = two_sum(row, total[t : t + 1])
            rest = rest + (extra + error[t : t + 1])
        results += [row, rest]
    return results


def rows_tile(rows):
    place = lax.broadcasted_iota(jnp.int32, (PAD, LANES), 0)
    tile = jnp.zeros((PAD, LANES), F32)
    for k, row in enumerate(rows):
        tile = jnp.where(place == k, row, tile)
    return tile


def exact_tile(tiles):
    total = tiles[0]
    error = jnp.zeros_like(total)
    for tile in tiles[1:]:
        total, extra = two_sum(total, tile)
        error = error + extra
    place = lax.broadcasted_iota(jnp.int32, (PAD, LANES), 0)
    errors = (place == 2) | (place == 4) | (place == 6)
    return total + jnp.where(errors, pltpu.roll(error, 1, 0), 0.0)


def is_packed(traits, share):
    return traits == 6 and share % (4 * LANES) == 0


def packed_width(traits, share):
    return share * 3 // 4 if is_packed(traits, share) else -(-share // LANES) * LANES


def spare_pieces(traits, share):
    main, rest = share * 3 // 4, share // 4
    return [
        (t, main, rest, traits + t // 3, t % 3 * rest)
        for t in range(traits if is_packed(traits, share) else 0)
    ]


def pack(out, i, values, traits, share):
    if not is_packed(traits, share):
        out[i, :, :share] = values
        return
    main = share * 3 // 4
    out[i, :traits, :main] = values[:traits, :main]
    for t, start, width, row, column in spare_pieces(traits, share):
        out[i, row : row + 1, column : column + width] = values[t : t + 1, start : start + width]


def totals_kernel(marker_weight, res_a, scal_a, res_m, scal_m, out, token):
    def pair(res_ref, scal_ref):
        res = res_ref[...]
        square = res * res
        return (
            jnp.sum(fold(square * scal_ref[...]), axis=0, keepdims=True),
            jnp.sum(fold(square), axis=0, keepdims=True),
        )

    product_a, norm_a = pair(res_a, scal_a)
    product_m, norm_m = pair(res_m, scal_m)
    tile = rows_tile([product_a + marker_weight * product_m, norm_a + marker_weight * norm_m])
    out[...] = jnp.broadcast_to(tile[None], out.shape)
    token[...] = tile


def prepare_kernel(
    bits,
    genotyped,
    token,
    res,
    scal,
    direction,
    send,
    row_index,
    res_m,
    scal_m,
    direction_m,
    search_out,
    direction_out,
    search_placed,
    direction_placed,
    search_ref,
    direction_ref,
    search_m,
    direction_m8,
):
    del token
    traits, animals = res.shape
    base = 1 << bits
    blocks = animals // base
    search_ref[...] = jnp.zeros_like(search_ref)
    direction_ref[...] = jnp.zeros_like(direction_ref)
    search_ref[:traits] = scal[...] * res[...]
    direction_ref[:traits] = direction[...]
    table = jnp.concatenate(
        [
            parts_of(ref[:, h * base : (h + 1) * base])
            for ref in (search_ref, direction_ref)
            for h in range(blocks)
        ],
        axis=0,
    ).astype(BF16)
    size = blocks * ROWS_EACH

    def one(r):
        index = send[pl.ds(r, 1), :]
        products = dot(table, one_hot(index & (base - 1), base))
        search_out[r] = select_blocks(products[:size], index >> bits, 0, blocks)
        direction_out[r] = select_blocks(products[size:], index >> bits, 0, blocks)

    if send.shape[0] <= 8:
        for r in range(send.shape[0]):
            one(r)
    else:
        pl.loop(0, send.shape[0])(one)

    blocks = -(-genotyped // (2 * base)) * 2
    width = 1024
    total = jnp.zeros((blocks * 2 * ROWS_EACH, base), F32)
    for start in range(0, animals, width):
        window = slice(start, start + width)
        index = row_index[:, window]
        parts = doubled_parts(search_ref[:, window]) + doubled_parts(direction_ref[:, window])
        total = total + dot_t(
            masked_blocks(parts, index >> bits, 0, blocks), one_hot(index & (base - 1), base)
        )
    for h in range(-(-genotyped // base)):
        size = min(base, genotyped - h * base)
        for k, out in enumerate((search_placed, direction_placed)):
            out[:, h * base : h * base + size] = block_of(total, h, 2, k)[:, :size]
    search_m[...] = jnp.zeros_like(search_m)
    direction_m8[...] = jnp.zeros_like(direction_m8)
    search_m[:traits] = scal_m[...] * res_m[...]
    direction_m8[:traits] = direction_m[...]


def animal_kernel(sums, previous, search, direction, search_out, direction_out, new_ref, out):
    conjugacy = product_of(sums) / previous[...]
    new_ref[...] = search[...] + conjugacy * direction[...]
    out[...] = search_out[...] + conjugacy.reshape(1, 1, 1) * direction_out[...]


def chunk_copies(genotypes, buffer, semaphores):
    width = buffer.shape[2]
    copies = [
        pltpu.make_async_copy(
            genotypes.at[:, i * width : (i + 1) * width], buffer.at[i], semaphores.at[i]
        )
        for i in range(buffer.shape[0])
    ]
    for copy in copies:
        copy.start()
    return copies


def predict_kernel(
    sums,
    previous,
    search,
    direction,
    genotypes,
    search_placed,
    direction_placed,
    new_m,
    out,
    buffer,
    semaphores,
):
    copies = chunk_copies(genotypes, buffer, semaphores)
    conjugacy = product_of(sums) / previous[...]
    new_m[...] = search[...] + conjugacy * direction[...]
    total = search_placed[...] + conjugacy * direction_placed[...]
    width = buffer.shape[2]
    for i, copy in enumerate(copies):
        new = new_m[:, i * width : (i + 1) * width].astype(BF16)
        copy.wait()
        total = total - dot_t(new, buffer[i])
    out[...] = total


def pedigree_kernel(bits, parents, new_a, sire, dam, sampling_ref, back_ref, left_ref):
    owners, _, base = parents.shape
    animals = new_a.shape[1]
    for h in range(0, owners, 2):
        left_ref[h * ROWS_EACH : (h + 2) * ROWS_EACH, :] = jnp.concatenate(
            [parts_of(parents[h]), parts_of(parents[h + 1])], axis=0
        ).astype(BF16)
    group = min(8, owners)
    groups = owners // group
    width = 1024
    slots = owners * base
    back_ref[...] = jnp.zeros_like(back_ref)
    for start in range(0, animals, width):
        window = slice(start, start + width)
        sire_index, dam_index = sire[:, window], dam[:, window]
        sire_high, dam_high = sire_index >> bits, dam_index >> bits
        sire_hot = one_hot(sire_index & (base - 1), base)
        dam_hot = one_hot(dam_index & (base - 1), base)
        gathered = jnp.zeros((PAD, width), F32)
        for g in range(groups):
            left = left_ref[g * group * ROWS_EACH : (g + 1) * group * ROWS_EACH, :]
            gathered = gathered + (
                select_blocks(dot(left, sire_hot), sire_high, g * group, group)
                + select_blocks(dot(left, dam_hot), dam_high, g * group, group)
            )
        known = (sire_index < slots).astype(F32) + (dam_index < slots).astype(F32)
        mendel = 1.0 / (1.0 - 0.25 * known)
        sampling = mendel * (new_a[:, window] - 0.5 * gathered)
        sampling_ref[:, window] = sampling
        parts = doubled_parts(-0.5 * sampling)
        for g in range(groups):
            total = dot_t(masked_blocks(parts, sire_high, g * group, group), sire_hot) + dot_t(
                masked_blocks(parts, dam_high, g * group, group), dam_hot
            )
            for h in range(group):
                back_ref[g * group + h] += block_of(total, h)


def deviation_kernel(share, traits, columns, *refs):
    deviation_body(share, traits, refs[:columns], *refs[columns:])


def deviation_body(
    share,
    traits,
    differences,
    genomic,
    genotypes,
    back,
    deviation_ref,
    out,
    genomic_ref,
    buffer,
    semaphores,
):
    copies = chunk_copies(genotypes, buffer, semaphores)
    load_matrix(genomic, genomic_ref)
    difference = differences[0][...]
    for other in differences[1:]:
        difference = difference + other[...]
    deviation = apply_matrix(genomic_ref, difference, traits)
    deviation_ref[...] = deviation
    rounded = deviation.astype(BF16)
    start = out.shape[2] - back.shape[2]
    out[:, :, start:] = back[...]
    per_chunk = buffer.shape[2] // share
    for i, copy in enumerate(copies):
        copy.wait()
        terms = dot(rounded, buffer[i])
        for j in range(per_chunk):
            pack(out, i * per_chunk + j, terms[:, j * share : (j + 1) * share], traits, share)


def record_kernel(token, sampling, new_a, pattern, table, genetic, out, matrix_ref):
    del token
    traits = genetic.shape[0]
    patterns = table.shape[1]
    load_matrix(genetic, matrix_ref)
    values = table[...]
    high = values.astype(BF16).astype(F32)
    rest = values - high
    middle = rest.astype(BF16).astype(F32)
    stacked = jnp.concatenate([high, middle, rest - middle], axis=0).astype(BF16)
    width = 1024
    size = traits * PAD
    for start in range(0, new_a.shape[1], width):
        window = slice(start, start + width)
        new = new_a[:, window]
        blocks = dot(stacked, one_hot(pattern[:, window], patterns))
        total = apply_matrix(matrix_ref, sampling[:, window], traits)
        for s in range(traits):
            row = slice(s * PAD, (s + 1) * PAD)
            block = blocks[row] + blocks[size:][row] + blocks[2 * size :][row]
            total = total + block * new[s : s + 1, :]
        out[:, window] = total


def image_kernel(
    bits,
    share,
    row,
    received,
    send,
    base_image,
    deviation,
    row_index,
    genetic,
    marker_inverse,
    new_a,
    res_a,
    new_share,
    res_share,
    image_a,
    out,
    matrix_ref,
    marker_ref,
    table_ref,
    terms_ref,
    res_ref,
):
    del row
    owners = received.shape[0]
    base = 1 << bits
    traits = genetic.shape[0]
    animals = base_image.shape[1]
    genotyped = deviation.shape[1]
    width = packed_width(traits, share)
    load_matrix(genetic, matrix_ref)
    load_matrix(marker_inverse, marker_ref)
    blocks = animals // base

    def scatter(r, total):
        index = send[pl.ds(r, 1), :]
        parts = doubled_parts(received[r, :, width:])
        return total + dot_t(
            masked_blocks(parts, index >> bits, 0, blocks), one_hot(index & (base - 1), base)
        )

    total = jnp.zeros((blocks * ROWS_EACH, base), F32)
    if owners <= 8:
        for r in range(owners):
            total = scatter(r, total)
    else:
        total = lax.fori_loop(0, owners, scatter, total)
    table_ref[...] = jnp.zeros_like(table_ref)
    table_ref[:, :genotyped] = deviation[...]
    places = table_ref.shape[1] // base
    table = jnp.concatenate(
        [parts_of(table_ref[:, h * base : (h + 1) * base]) for h in range(places)], axis=0
    ).astype(BF16)
    for h in range(blocks):
        window = slice(h * base, (h + 1) * base)
        index = row_index[:, window]
        gathered = block_of(total, h)
        genomic_term = select_blocks(
            dot(table, one_hot(index & (base - 1), base)), index >> bits, 0, places
        )
        image_a[:, window] = (
            base_image[:, window] + apply_matrix(matrix_ref, gathered, traits) + genomic_term
        )

    summed = received[0, :, :width]
    for i in range(1, owners):
        summed = summed + received[i, :, :width]
    terms_ref[...] = jnp.zeros_like(terms_ref)
    res_ref[...] = jnp.zeros_like(res_ref)
    res_ref[:traits, :share] = res_share[...]
    if is_packed(traits, share):
        main = share * 3 // 4
        terms_ref[:traits, :main] = summed[:traits, :main]
        for t, start, size, place, column in spare_pieces(traits, share):
            terms_ref[t : t + 1, start : start + size] = summed[
                place : place + 1, column : column + size
            ]
    else:
        terms_ref[:, :width] = summed
    new = new_share[...]
    image = apply_matrix(marker_ref, new, traits) - terms_ref[:, :share]
    terms_ref[:, :share] = image
    curvature = fold(new_a[...] * image_a[...])
    if share % LANES == 0:
        curvature = curvature + fold(new * image)
        curvature = jnp.sum(curvature, axis=0, keepdims=True)
    else:
        rest = jnp.sum(jnp.sum(new * image, axis=1, keepdims=True), axis=0, keepdims=True)
        first = lax.broadcasted_iota(jnp.int32, (1, LANES), 1) == 0
        curvature = jnp.sum(curvature, axis=0, keepdims=True) + jnp.where(first, rest, 0.0)
    tile = rows_tile(
        [curvature]
        + exact_sums(
            [
                (res_a[...], image_a[:traits]),
                (res_ref[:traits], terms_ref[:traits]),
            ]
        )
    )
    for i in range(owners):
        if not is_packed(traits, share):
            out[i] = jnp.zeros(out.shape[1:], F32)
        pack(out, i, image, traits, share)
        out[i, :, width:] = tile


def spread_kernel(received, out):
    start = received.shape[2] - LANES
    tile = exact_tile([received[i, :, start:] for i in range(received.shape[0])])
    out[...] = tile


def final_kernel(
    share,
    columns,
    sums,
    *refs,
):
    tiles = refs[:columns]
    final_body(share, sums, tiles, *refs[columns:])


def final_body(
    share,
    sums,
    tiles,
    sol_a,
    res_a,
    new_a,
    image_a,
    sol_m,
    res_m,
    new_m,
    gathered,
    next_sol_a,
    next_sol_m,
    next_res_a,
    next_res_m,
    reduction,
):
    traits = sol_a.shape[0]
    tile = exact_tile([ref[...] for ref in tiles])
    step = product_of(sums) / jnp.sum(tile[0:1], axis=1, keepdims=True)
    next_sol_a[...] = sol_a[...] + step * new_a[:traits]
    next_res_a[...] = res_a[...] - step * image_a[:traits]
    next_sol_m[...] = sol_m[...] + step * new_m[:traits]
    for i in range(gathered.shape[0]):
        left = i * share
        if is_packed(traits, share):
            main = share * 3 // 4
            window = slice(left, left + main)
            next_res_m[:, window] = res_m[:, window] - step * gathered[i, :traits, :main]
            for t, start, size, place, column in spare_pieces(traits, share):
                window = slice(left + start, left + start + size)
                next_res_m[t : t + 1, window] = (
                    res_m[t : t + 1, window]
                    - step * gathered[i, place : place + 1, column : column + size]
                )
        else:
            window = slice(left, left + share)
            next_res_m[:, window] = res_m[:, window] - step * gathered[i, :traits, :share]

    step_row = jnp.broadcast_to(step, (1, LANES))
    step_halves = halves(step_row)

    def times_step(total, error):
        product, rounding = two_product(total, halves(total), step_row, step_halves)
        return product, rounding + error * step_row

    cross, cross_error = times_step(tile[3:4], tile[4:5])
    square, square_error = times_step(*times_step(tile[5:6], tile[6:7]))
    total, first = two_sum(tile[1:2], -2.0 * cross)
    total, second = two_sum(total, square)
    norm = total + (first + second + tile[2:3] - 2.0 * cross_error + square_error)
    reduction[...] = jnp.sum(norm, axis=1, keepdims=True) / norm_of(sums)


def exchange(values, axes):
    return lax.all_to_all(values, axes, split_axis=0, concat_axis=0, tiled=True)


def copies_of(values, axis):
    size = lax.axis_size(axis)
    return [values] + [
        lax.ppermute(values, axis, [(i, i ^ k) for i in range(size)])
        for k in range(1, size)
    ]


def local(
    solution_animal,
    solution_marker,
    residual_animal,
    residual_marker,
    direction_animal,
    direction_marker,
    scaling_animal,
    scaling_marker,
    previous_product,
    genotypes,
    genetic_inverse,
    genomic_inverse,
    marker_inverse,
    residual_table,
    pattern,
    sire_slot,
    dam_slot,
    genotype_row,
    send_list,
):
    traits, animals = residual_animal.shape
    markers = residual_marker.shape[1]
    genotyped = genotypes.shape[0]
    rows = lax.axis_size("rows")
    columns = lax.axis_size("mk")
    capacity = send_list.shape[3]
    bits = capacity.bit_length() - 1
    share = markers // rows
    patterns = residual_table.shape[0]
    row = lax.axis_index("rows").astype(jnp.int32).reshape(1)
    previous = previous_product.reshape(1, 1)
    send = send_list.reshape(rows, capacity)
    sire, dam = sire_slot.reshape(1, animals), dam_slot.reshape(1, animals)
    kinds, places = pattern.reshape(1, animals), genotype_row.reshape(1, animals)
    def hbm(*arrays):
        return [pltpu.with_memory_space_constraint(array, pltpu.HBM) for array in arrays]

    animal_block = shape_of(PAD, animals)
    slot_block = shape_of(rows, PAD, capacity)
    tile = shape_of(PAD, LANES)
    local_sums, token = call(
        functools.partial(totals_kernel, 1.0 / rows),
        (shape_of(rows * columns, PAD, LANES), tile),
        name="totals",
    )(*hbm(residual_animal, scaling_animal, residual_marker, scaling_marker))
    sums = exchange(local_sums, ("rows", "mk"))
    in_vmem, in_hbm = pl.BlockSpec(memory_space=pltpu.VMEM), pl.BlockSpec(memory_space=pl.ANY)

    placed_block, marker_block = shape_of(PAD, genotyped), shape_of(PAD, markers)
    (
        search_out,
        direction_out,
        search_placed,
        direction_placed,
        search_animal,
        padded_direction,
        search_marker,
        padded_marker,
    ) = call(
        functools.partial(prepare_kernel, bits, genotyped),
        (slot_block, slot_block, placed_block, placed_block)
        + (animal_block, animal_block, marker_block, marker_block),
        name="prepare",
    )(
        token,
        *hbm(residual_animal, scaling_animal, direction_animal, send, places),
        *hbm(residual_marker, scaling_marker, direction_marker),
    )
    new_animal, outgoing = call(animal_kernel, (animal_block, slot_block), name="animals")(
        sums, previous, search_animal, padded_direction, search_out, direction_out
    )
    parents = exchange(outgoing, "rows")

    (genotypes,) = hbm(genotypes)

    def chunks(width):
        return (
            pltpu.VMEM((markers // width, genotyped, width), BF16),
            pltpu.SemaphoreType.DMA((markers // width,)),
        )

    chunk = share * max(1, 1536 // share)
    new_marker, difference = call(
        predict_kernel,
        (marker_block, placed_block),
        chunks(2 * chunk),
        in_specs=[in_vmem] * 4 + [in_hbm] + [in_vmem] * 2,
        name="predict",
    )(
        sums,
        previous,
        search_marker,
        padded_marker,
        genotypes,
        search_placed,
        direction_placed,
    )
    differences = copies_of(difference, "mk")
    sampling, back = call(
        functools.partial(pedigree_kernel, bits),
        (animal_block, slot_block),
        (pltpu.VMEM((rows * ROWS_EACH, capacity), BF16),),
        name="pedigree",
    )(parents, new_animal, sire, dam)
    width = packed_width(traits, share)
    deviation, payload = call(
        functools.partial(deviation_kernel, share, traits, columns),
        (placed_block, shape_of(rows, PAD, width + capacity)),
        (pltpu.VMEM((PAD, LANES), F32), *chunks(chunk)),
        in_specs=[in_vmem] * (columns + 1) + [in_hbm, in_vmem],
        name="deviation",
    )(*differences, genomic_inverse, genotypes, back)
    received = exchange(payload, "rows")
    residual_table, deviation = lax.optimization_barrier((residual_table, deviation))
    table = jnp.pad(jnp.transpose(residual_table, (2, 1, 0)), ((0, 0), (0, PAD - traits), (0, 0)))
    table = table.reshape(traits * PAD, patterns)
    base_image = call(record_kernel, animal_block, (pltpu.VMEM((PAD, LANES), F32),), name="record")(
        deviation, sampling, new_animal, kinds, table, genetic_inverse
    )

    if share % LANES:
        start = row[0] * share
        new_share = lax.dynamic_slice_in_dim(new_marker, start, share, 1)
        res_share = lax.dynamic_slice_in_dim(residual_marker, start, share, 1)

        def own(height):
            return pl.BlockSpec((height, share), lambda k, r: (0, 0))
    else:
        new_share, res_share = new_marker, residual_marker

        def own(height):
            return pl.BlockSpec((height, share), lambda k, r: (0, r[0]))

    def still(array):
        return pl.BlockSpec(array.shape, lambda k, r, n=len(array.shape): (0,) * n)

    out_shape = shape_of(rows, PAD, width + LANES)
    full = -(-share // LANES) * LANES
    inputs = (
        received,
        send,
        base_image,
        deviation,
        places,
        genetic_inverse,
        marker_inverse,
        new_animal,
        residual_animal,
    )
    image_animal, payload = pl.pallas_call(
        functools.partial(image_kernel, bits, share),
        out_shape=(animal_block, out_shape),
        grid_spec=pltpu.PrefetchScalarGridSpec(
            num_scalar_prefetch=1,
            grid=(1,),
            in_specs=[still(array) for array in inputs] + [own(PAD), own(traits)],
            out_specs=(still(animal_block), still(out_shape)),
            scratch_shapes=[
                pltpu.VMEM((PAD, LANES), F32),
                pltpu.VMEM((PAD, LANES), F32),
                pltpu.VMEM((PAD, -(-genotyped // capacity) * capacity), F32),
                pltpu.VMEM((PAD, full), F32),
                pltpu.VMEM((PAD, full), F32),
            ],
        ),
        compiler_params=LIMIT,
        name="image",
    )(row, *inputs, new_share, res_share)
    gathered = exchange(payload, "rows")
    tiles = copies_of(call(spread_kernel, tile, name="spread")(gathered), "mk")
    *outputs, reduction = call(
        functools.partial(final_kernel, share, columns),
        (
            shape_of(traits, animals),
            shape_of(traits, markers),
            shape_of(traits, animals),
            shape_of(traits, markers),
            shape_of(1, 1),
        ),
        name="final",
    )(
        sums,
        *tiles,
        solution_animal,
        residual_animal,
        new_animal,
        image_animal,
        solution_marker,
        residual_marker,
        new_marker,
        gathered,
    )
    return (*outputs, reduction.reshape(()))


def solution(mesh):
    animal, marker = P(None, ("rows", "mk")), P(None, "mk")
    index = P(("rows", "mk"))
    return jax.shard_map(
        local,
        mesh=mesh,
        in_specs=(
            animal,
            marker,
            animal,
            marker,
            animal,
            marker,
            animal,
            marker,
            P(),
            P("rows", "mk"),
            P(),
            P(),
            P(),
            P(),
            index,
            index,
            index,
            index,
            P("rows", "mk", None, None),
        ),
        out_specs=(animal, marker, animal, marker, P()),
        check_vma=False,
    )
```

```python
import functools

import jax
import jax.numpy as jnp
from jax import lax
from jax.experimental import pallas as pl
from jax.experimental.pallas import tpu as pltpu
from jax.sharding import PartitionSpec as P

F32 = jnp.float32
BF16 = jnp.bfloat16
PAD = 8
LANES = 128


def shape_of(*dims, dtype=F32):
    return jax.ShapeDtypeStruct(dims, dtype)


KEPT = 128
LIMIT = pltpu.CompilerParams(vmem_limit_bytes=24 << 20)


def call(kernel, out_shape, scratch=(), **options):
    return pl.pallas_call(
        kernel,
        out_shape=out_shape,
        scratch_shapes=list(scratch),
        compiler_params=LIMIT,
        **options,
    )


def parts_of(values):
    high = values.astype(BF16).astype(F32)
    rest = values - high
    middle = rest.astype(BF16).astype(F32)
    return jnp.concatenate([high, middle, rest - middle], axis=0)


def add_parts(stacked):
    return stacked[:PAD] + stacked[PAD : 2 * PAD] + stacked[2 * PAD :]


ROWS_EACH = 3 * PAD


def one_hot(low, base):
    wanted = lax.broadcasted_iota(jnp.int32, (base, LANES), 0).astype(F32).astype(BF16)
    wanted = jnp.concatenate([wanted] * (low.shape[1] // LANES), axis=1)
    found = wanted == low.astype(F32).astype(BF16)
    return jnp.where(found, jnp.ones((), BF16), jnp.zeros((), BF16))


def dot(left, right):
    return lax.dot_general(left, right, (((1,), (0,)), ((), ())), preferred_element_type=F32)


def dot_t(left, right):
    return lax.dot_general(left, right, (((1,), (1,)), ((), ())), preferred_element_type=F32)


def select_blocks(products, high, first, count):
    total = None
    for h in range(count):
        block = add_parts(products[h * ROWS_EACH : (h + 1) * ROWS_EACH])
        block = jnp.where(high == first + h, block, 0.0)
        total = block if total is None else total + block
    return total


def doubled_parts(values):
    stacked = parts_of(values)
    parts = [stacked[p * PAD : (p + 1) * PAD] for p in range(3)]
    return [jnp.concatenate([part, part], axis=0).astype(BF16) for part in parts]


def masked_blocks(parts, high, first, count):
    half = lax.broadcasted_iota(jnp.int32, (2 * PAD, LANES), 0) // PAD
    half = half.astype(F32).astype(BF16)
    half = jnp.concatenate([half] * (high.shape[1] // LANES), axis=1)
    tiles = []
    for pair in range(0, count, 2):
        found = half == (high - (first + pair)).astype(F32).astype(BF16)
        tiles += [jnp.where(found, part, jnp.zeros((), BF16)) for part in parts]
    return jnp.concatenate(tiles, axis=0)


def block_of(total, h, kinds=1, kind=0):
    start = (h // 2 * kinds + kind) * 3 * 2 * PAD + h % 2 * PAD
    rows = [total[start + p * 2 * PAD : start + p * 2 * PAD + PAD] for p in range(3)]
    return rows[0] + rows[1] + rows[2]


def fold(values):
    total = values[:, :LANES]
    for start in range(LANES, values.shape[1], LANES):
        total = total + values[:, start : start + LANES]
    return total


def load_matrix(matrix_ref, padded_ref):
    padded_ref[...] = jnp.zeros_like(padded_ref)
    size = matrix_ref.shape[0]
    padded_ref[:size, :size] = matrix_ref[...]


def apply_matrix(padded_ref, values, count):
    total = None
    for s in range(count):
        term = padded_ref[:, s : s + 1] * values[s : s + 1, :]
        total = term if total is None else total + term
    return total


def sums_of(received_ref):
    tile = received_ref[0]
    for i in range(1, received_ref.shape[0]):
        tile = tile + received_ref[i]
    return tile


def product_of(sums_ref):
    return jnp.sum(sums_of(sums_ref)[0:1], axis=1, keepdims=True)


def norm_of(sums_ref):
    return jnp.sum(sums_of(sums_ref)[1:2], axis=1, keepdims=True)


def two_sum(left, right):
    total = left + right
    back = total - left
    return total, (left - (total - back)) + (right - back)


def halves(values):
    scaled = values * 4097.0
    high = scaled - (scaled - values)
    return high, values - high


def two_product(left, left_halves, right, right_halves):
    product = left * right
    (lh, ll), (rh, rl) = left_halves, right_halves
    return product, ((lh * rh - product) + lh * rl + ll * rh) + ll * rl


def exact_sums(pairs):
    columns = []
    for left, right in pairs:
        lh, rh = halves(left), halves(right)
        for a, ah, b, bh in ((left, lh, left, lh), (left, lh, right, rh), (right, rh, right, rh)):
            columns.append(two_product(a, ah, b, bh))
    results = []
    for kind in range(3):
        total = error = None
        for product, rounding in columns[kind::3]:
            for start in range(0, product.shape[1], LANES):
                window = slice(start, start + LANES)
                if total is None:
                    total, error = product[:, window], rounding[:, window]
                else:
                    total, extra = two_sum(total, product[:, window])
                    error = error + (extra + rounding[:, window])
        row, rest = total[0:1], error[0:1]
        for t in range(1, total.shape[0]):
            row, extra = two_sum(row, total[t : t + 1])
            rest = rest + (extra + error[t : t + 1])
        results += [row, rest]
    return results


def rows_tile(rows):
    place = lax.broadcasted_iota(jnp.int32, (PAD, LANES), 0)
    tile = jnp.zeros((PAD, LANES), F32)
    for k, row in enumerate(rows):
        tile = jnp.where(place == k, row, tile)
    return tile


def exact_tile(tiles):
    total = tiles[0]
    error = jnp.zeros_like(total)
    for tile in tiles[1:]:
        total, extra = two_sum(total, tile)
        error = error + extra
    place = lax.broadcasted_iota(jnp.int32, (PAD, LANES), 0)
    errors = (place == 2) | (place == 4) | (place == 6)
    return total + jnp.where(errors, pltpu.roll(error, 1, 0), 0.0)


def is_packed(traits, share):
    return traits == 6 and share % (4 * LANES) == 0


def packed_width(traits, share):
    return share * 3 // 4 if is_packed(traits, share) else -(-share // LANES) * LANES


def spare_pieces(traits, share):
    main, rest = share * 3 // 4, share // 4
    return [
        (t, main, rest, traits + t // 3, t % 3 * rest)
        for t in range(traits if is_packed(traits, share) else 0)
    ]


def pack(out, i, values, traits, share):
    if not is_packed(traits, share):
        out[i, :, :share] = values
        return
    main = share * 3 // 4
    out[i, :traits, :main] = values[:traits, :main]
    for t, start, width, row, column in spare_pieces(traits, share):
        out[i, row : row + 1, column : column + width] = values[t : t + 1, start : start + width]


def totals_kernel(marker_weight, res_a, scal_a, res_m, scal_m, out, token):
    def pair(res_ref, scal_ref):
        res = res_ref[...]
        square = res * res
        return (
            jnp.sum(fold(square * scal_ref[...]), axis=0, keepdims=True),
            jnp.sum(fold(square), axis=0, keepdims=True),
        )

    product_a, norm_a = pair(res_a, scal_a)
    product_m, norm_m = pair(res_m, scal_m)
    tile = rows_tile([product_a + marker_weight * product_m, norm_a + marker_weight * norm_m])
    out[...] = jnp.broadcast_to(tile[None], out.shape)
    token[...] = tile


def prepare_kernel(
    bits,
    genotyped,
    token,
    res,
    scal,
    direction,
    send,
    row_index,
    res_m,
    scal_m,
    direction_m,
    search_out,
    direction_out,
    search_placed,
    direction_placed,
    search_ref,
    direction_ref,
    search_m,
    direction_m8,
):
    del token
    traits, animals = res.shape
    base = 1 << bits
    blocks = animals // base
    search_ref[...] = jnp.zeros_like(search_ref)
    direction_ref[...] = jnp.zeros_like(direction_ref)
    search_ref[:traits] = scal[...] * res[...]
    direction_ref[:traits] = direction[...]
    table = jnp.concatenate(
        [
            parts_of(ref[:, h * base : (h + 1) * base])
            for ref in (search_ref, direction_ref)
            for h in range(blocks)
        ],
        axis=0,
    ).astype(BF16)
    size = blocks * ROWS_EACH

    def one(r):
        index = send[pl.ds(r, 1), :]
        products = dot(table, one_hot(index & (base - 1), base))
        search_out[r] = select_blocks(products[:size], index >> bits, 0, blocks)
        direction_out[r] = select_blocks(products[size:], index >> bits, 0, blocks)

    if send.shape[0] <= 8:
        for r in range(send.shape[0]):
            one(r)
    else:
        pl.loop(0, send.shape[0])(one)

    blocks = -(-genotyped // (2 * base)) * 2
    width = 1024
    total = jnp.zeros((blocks * 2 * ROWS_EACH, base), F32)
    for start in range(0, animals, width):
        window = slice(start, start + width)
        index = row_index[:, window]
        parts = doubled_parts(search_ref[:, window]) + doubled_parts(direction_ref[:, window])
        total = total + dot_t(
            masked_blocks(parts, index >> bits, 0, blocks), one_hot(index & (base - 1), base)
        )
    for h in range(-(-genotyped // base)):
        size = min(base, genotyped - h * base)
        for k, out in enumerate((search_placed, direction_placed)):
            out[:, h * base : h * base + size] = block_of(total, h, 2, k)[:, :size]
    search_m[...] = jnp.zeros_like(search_m)
    direction_m8[...] = jnp.zeros_like(direction_m8)
    search_m[:traits] = scal_m[...] * res_m[...]
    direction_m8[:traits] = direction_m[...]


def animal_kernel(sums, previous, search, direction, search_out, direction_out, new_ref, out):
    conjugacy = product_of(sums) / previous[...]
    new_ref[...] = search[...] + conjugacy * direction[...]
    out[...] = search_out[...] + conjugacy.reshape(1, 1, 1) * direction_out[...]


def chunk_copies(genotypes, buffer, semaphores):
    width = buffer.shape[2]
    first = genotypes.shape[0] - buffer.shape[1]
    copies = [
        pltpu.make_async_copy(
            genotypes.at[first:, i * width : (i + 1) * width], buffer.at[i], semaphores.at[i]
        )
        for i in range(buffer.shape[0])
    ]
    for copy in copies:
        copy.start()
    return copies


def predict_kernel(
    sums,
    previous,
    search,
    direction,
    genotypes,
    search_placed,
    direction_placed,
    new_m,
    out,
    buffer,
    semaphores,
):
    copies = chunk_copies(genotypes, buffer, semaphores)
    conjugacy = product_of(sums) / previous[...]
    new_m[...] = search[...] + conjugacy * direction[...]
    total = search_placed[...] + conjugacy * direction_placed[...]
    width = buffer.shape[2]
    for i, copy in enumerate(copies):
        new = new_m[:, i * width : (i + 1) * width].astype(BF16)
        copy.wait()
        total = total - dot_t(new, buffer[i])
    out[...] = total


def pedigree_kernel(
    bits,
    parents,
    new_a,
    sire,
    dam,
    genotypes,
    sampling_ref,
    back_ref,
    resident,
    left_ref,
    semaphore,
):
    copy = pltpu.make_async_copy(genotypes.at[: resident.shape[0]], resident, semaphore)
    copy.start()
    owners, _, base = parents.shape
    animals = new_a.shape[1]
    for h in range(0, owners, 2):
        left_ref[h * ROWS_EACH : (h + 2) * ROWS_EACH, :] = jnp.concatenate(
            [parts_of(parents[h]), parts_of(parents[h + 1])], axis=0
        ).astype(BF16)
    group = min(8, owners)
    groups = owners // group
    width = 1024
    slots = owners * base
    back_ref[...] = jnp.zeros_like(back_ref)
    for start in range(0, animals, width):
        window = slice(start, start + width)
        sire_index, dam_index = sire[:, window], dam[:, window]
        sire_high, dam_high = sire_index >> bits, dam_index >> bits
        sire_hot = one_hot(sire_index & (base - 1), base)
        dam_hot = one_hot(dam_index & (base - 1), base)
        gathered = jnp.zeros((PAD, width), F32)
        for g in range(groups):
            left = left_ref[g * group * ROWS_EACH : (g + 1) * group * ROWS_EACH, :]
            gathered = gathered + (
                select_blocks(dot(left, sire_hot), sire_high, g * group, group)
                + select_blocks(dot(left, dam_hot), dam_high, g * group, group)
            )
        known = (sire_index < slots).astype(F32) + (dam_index < slots).astype(F32)
        mendel = 1.0 / (1.0 - 0.25 * known)
        sampling = mendel * (new_a[:, window] - 0.5 * gathered)
        sampling_ref[:, window] = sampling
        parts = doubled_parts(-0.5 * sampling)
        for g in range(groups):
            total = dot_t(masked_blocks(parts, sire_high, g * group, group), sire_hot) + dot_t(
                masked_blocks(parts, dam_high, g * group, group), dam_hot
            )
            for h in range(group):
                back_ref[g * group + h] += block_of(total, h)
    copy.wait()


def deviation_kernel(share, traits, columns, *refs):
    deviation_body(share, traits, refs[:columns], *refs[columns:])


def deviation_body(
    share,
    traits,
    differences,
    genomic,
    resident,
    genotypes,
    back,
    deviation_ref,
    out,
    genomic_ref,
    buffer,
    semaphores,
):
    copies = chunk_copies(genotypes, buffer, semaphores)
    load_matrix(genomic, genomic_ref)
    difference = differences[0][...]
    for other in differences[1:]:
        difference = difference + other[...]
    deviation = apply_matrix(genomic_ref, difference, traits)
    deviation_ref[...] = deviation
    rounded = deviation.astype(BF16)
    start = out.shape[2] - back.shape[2]
    out[:, :, start:] = back[...]
    per_chunk = buffer.shape[2] // share
    first = resident.shape[0]
    for i, copy in enumerate(copies):
        width = buffer.shape[2]
        terms = dot(rounded[:, :first], resident[:, i * width : (i + 1) * width])
        copy.wait()
        terms = terms + dot(rounded[:, first:], buffer[i])
        for j in range(per_chunk):
            pack(out, i * per_chunk + j, terms[:, j * share : (j + 1) * share], traits, share)


def record_kernel(
    bits,
    deviation,
    sampling,
    new_a,
    pattern,
    row_index,
    table,
    genetic,
    out,
    matrix_ref,
    table_ref,
):
    traits = genetic.shape[0]
    base = 1 << bits
    table_ref[...] = jnp.zeros_like(table_ref)
    table_ref[:, : deviation.shape[1]] = deviation[...]
    places = table_ref.shape[1] // base
    genomic = jnp.concatenate(
        [parts_of(table_ref[:, h * base : (h + 1) * base]) for h in range(places)], axis=0
    ).astype(BF16)
    patterns = table.shape[1]
    load_matrix(genetic, matrix_ref)
    values = table[...]
    high = values.astype(BF16).astype(F32)
    rest = values - high
    middle = rest.astype(BF16).astype(F32)
    stacked = jnp.concatenate([high, middle, rest - middle], axis=0).astype(BF16)
    width = 1024
    size = traits * PAD
    for start in range(0, new_a.shape[1], width):
        window = slice(start, start + width)
        new = new_a[:, window]
        blocks = dot(stacked, one_hot(pattern[:, window], patterns))
        total = apply_matrix(matrix_ref, sampling[:, window], traits)
        for s in range(traits):
            row = slice(s * PAD, (s + 1) * PAD)
            block = blocks[row] + blocks[size:][row] + blocks[2 * size :][row]
            total = total + block * new[s : s + 1, :]
        index = row_index[:, window]
        products = dot(genomic, one_hot(index & (base - 1), base))
        out[:, window] = total + select_blocks(products, index >> bits, 0, places)


def image_kernel(
    bits,
    share,
    row,
    received,
    send,
    base_image,
    genetic,
    marker_inverse,
    new_a,
    res_a,
    new_share,
    res_share,
    image_a,
    out,
    matrix_ref,
    marker_ref,
    terms_ref,
    res_ref,
):
    del row
    owners = received.shape[0]
    base = 1 << bits
    traits = genetic.shape[0]
    animals = base_image.shape[1]
    width = packed_width(traits, share)
    load_matrix(genetic, matrix_ref)
    load_matrix(marker_inverse, marker_ref)
    blocks = animals // base

    def scatter(r, total):
        index = send[pl.ds(r, 1), :]
        parts = doubled_parts(received[r, :, width:])
        return total + dot_t(
            masked_blocks(parts, index >> bits, 0, blocks), one_hot(index & (base - 1), base)
        )

    total = jnp.zeros((blocks * ROWS_EACH, base), F32)
    if owners <= 8:
        for r in range(owners):
            total = scatter(r, total)
    else:
        total = lax.fori_loop(0, owners, scatter, total)
    for h in range(blocks):
        window = slice(h * base, (h + 1) * base)
        gathered = block_of(total, h)
        image_a[:, window] = base_image[:, window] + apply_matrix(matrix_ref, gathered, traits)

    summed = received[0, :, :width]
    for i in range(1, owners):
        summed = summed + received[i, :, :width]
    terms_ref[...] = jnp.zeros_like(terms_ref)
    res_ref[...] = jnp.zeros_like(res_ref)
    res_ref[:traits, :share] = res_share[...]
    if is_packed(traits, share):
        main = share * 3 // 4
        terms_ref[:traits, :main] = summed[:traits, :main]
        for t, start, size, place, column in spare_pieces(traits, share):
            terms_ref[t : t + 1, start : start + size] = summed[
                place : place + 1, column : column + size
            ]
    else:
        terms_ref[:, :width] = summed
    new = new_share[...]
    image = apply_matrix(marker_ref, new, traits) - terms_ref[:, :share]
    terms_ref[:, :share] = image
    curvature = fold(new_a[...] * image_a[...])
    if share % LANES == 0:
        curvature = curvature + fold(new * image)
        curvature = jnp.sum(curvature, axis=0, keepdims=True)
    else:
        rest = jnp.sum(jnp.sum(new * image, axis=1, keepdims=True), axis=0, keepdims=True)
        first = lax.broadcasted_iota(jnp.int32, (1, LANES), 1) == 0
        curvature = jnp.sum(curvature, axis=0, keepdims=True) + jnp.where(first, rest, 0.0)
    tile = rows_tile(
        [curvature]
        + exact_sums(
            [
                (res_a[...], image_a[:traits]),
                (res_ref[:traits], terms_ref[:traits]),
            ]
        )
    )
    for i in range(owners):
        if not is_packed(traits, share):
            out[i] = jnp.zeros(out.shape[1:], F32)
        pack(out, i, image, traits, share)
        out[i, :, width:] = tile


def spread_kernel(received, out):
    start = received.shape[2] - LANES
    tile = exact_tile([received[i, :, start:] for i in range(received.shape[0])])
    out[...] = tile


def final_kernel(
    share,
    columns,
    sums,
    *refs,
):
    tiles = refs[:columns]
    final_body(share, sums, tiles, *refs[columns:])


def final_body(
    share,
    sums,
    tiles,
    sol_a,
    res_a,
    new_a,
    image_a,
    sol_m,
    res_m,
    new_m,
    gathered,
    next_sol_a,
    next_sol_m,
    next_res_a,
    next_res_m,
    reduction,
):
    traits = sol_a.shape[0]
    tile = exact_tile([ref[...] for ref in tiles])
    step = product_of(sums) / jnp.sum(tile[0:1], axis=1, keepdims=True)
    next_sol_a[...] = sol_a[...] + step * new_a[:traits]
    next_res_a[...] = res_a[...] - step * image_a[:traits]
    next_sol_m[...] = sol_m[...] + step * new_m[:traits]
    for i in range(gathered.shape[0]):
        left = i * share
        if is_packed(traits, share):
            main = share * 3 // 4
            window = slice(left, left + main)
            next_res_m[:, window] = res_m[:, window] - step * gathered[i, :traits, :main]
            for t, start, size, place, column in spare_pieces(traits, share):
                window = slice(left + start, left + start + size)
                next_res_m[t : t + 1, window] = (
                    res_m[t : t + 1, window]
                    - step * gathered[i, place : place + 1, column : column + size]
                )
        else:
            window = slice(left, left + share)
            next_res_m[:, window] = res_m[:, window] - step * gathered[i, :traits, :share]

    step_row = jnp.broadcast_to(step, (1, LANES))
    step_halves = halves(step_row)

    def times_step(total, error):
        product, rounding = two_product(total, halves(total), step_row, step_halves)
        return product, rounding + error * step_row

    cross, cross_error = times_step(tile[3:4], tile[4:5])
    square, square_error = times_step(*times_step(tile[5:6], tile[6:7]))
    total, first = two_sum(tile[1:2], -2.0 * cross)
    total, second = two_sum(total, square)
    norm = total + (first + second + tile[2:3] - 2.0 * cross_error + square_error)
    reduction[...] = jnp.sum(norm, axis=1, keepdims=True) / norm_of(sums)


def exchange(values, axes):
    return lax.all_to_all(values, axes, split_axis=0, concat_axis=0, tiled=True)


def copies_of(values, axis):
    size = lax.axis_size(axis)
    return [values] + [
        lax.ppermute(values, axis, [(i, i ^ k) for i in range(size)])
        for k in range(1, size)
    ]


def local(
    solution_animal,
    solution_marker,
    residual_animal,
    residual_marker,
    direction_animal,
    direction_marker,
    scaling_animal,
    scaling_marker,
    previous_product,
    genotypes,
    genetic_inverse,
    genomic_inverse,
    marker_inverse,
    residual_table,
    pattern,
    sire_slot,
    dam_slot,
    genotype_row,
    send_list,
):
    traits, animals = residual_animal.shape
    markers = residual_marker.shape[1]
    genotyped = genotypes.shape[0]
    rows = lax.axis_size("rows")
    columns = lax.axis_size("mk")
    capacity = send_list.shape[3]
    bits = capacity.bit_length() - 1
    share = markers // rows
    patterns = residual_table.shape[0]
    row = lax.axis_index("rows").astype(jnp.int32).reshape(1)
    previous = previous_product.reshape(1, 1)
    send = send_list.reshape(rows, capacity)
    sire, dam = sire_slot.reshape(1, animals), dam_slot.reshape(1, animals)
    kinds, places = pattern.reshape(1, animals), genotype_row.reshape(1, animals)
    def hbm(*arrays):
        return [pltpu.with_memory_space_constraint(array, pltpu.HBM) for array in arrays]

    animal_block = shape_of(PAD, animals)
    slot_block = shape_of(rows, PAD, capacity)
    tile = shape_of(PAD, LANES)
    local_sums, token = call(
        functools.partial(totals_kernel, 1.0 / rows),
        (shape_of(rows * columns, PAD, LANES), tile),
        name="totals",
    )(*hbm(residual_animal, scaling_animal, residual_marker, scaling_marker))
    sums = exchange(local_sums, ("rows", "mk"))
    in_vmem, in_hbm = pl.BlockSpec(memory_space=pltpu.VMEM), pl.BlockSpec(memory_space=pl.ANY)

    placed_block, marker_block = shape_of(PAD, genotyped), shape_of(PAD, markers)
    (
        search_out,
        direction_out,
        search_placed,
        direction_placed,
        search_animal,
        padded_direction,
        search_marker,
        padded_marker,
    ) = call(
        functools.partial(prepare_kernel, bits, genotyped),
        (slot_block, slot_block, placed_block, placed_block)
        + (animal_block, animal_block, marker_block, marker_block),
        name="prepare",
    )(
        token,
        *hbm(residual_animal, scaling_animal, direction_animal, send, places),
        *hbm(residual_marker, scaling_marker, direction_marker),
    )
    new_animal, outgoing = call(animal_kernel, (animal_block, slot_block), name="animals")(
        sums, previous, search_animal, padded_direction, search_out, direction_out
    )
    parents = exchange(outgoing, "rows")

    (genotypes,) = hbm(genotypes)

    def chunks(width, kept):
        return (
            pltpu.VMEM((markers // width, genotyped - kept, width), BF16),
            pltpu.SemaphoreType.DMA((markers // width,)),
        )

    chunk = share * max(1, 1536 // share)
    new_marker, difference = call(
        predict_kernel,
        (marker_block, placed_block),
        chunks(2 * chunk, 0),
        in_specs=[in_vmem] * 4 + [in_hbm] + [in_vmem] * 2,
        name="predict",
    )(
        sums,
        previous,
        search_marker,
        padded_marker,
        genotypes,
        search_placed,
        direction_placed,
    )
    differences = copies_of(difference, "mk")
    sampling, back, resident = call(
        functools.partial(pedigree_kernel, bits),
        (animal_block, slot_block, pltpu.VMEM((KEPT, markers), BF16)),
        (pltpu.VMEM((rows * ROWS_EACH, capacity), BF16), pltpu.SemaphoreType.DMA),
        in_specs=[in_vmem] * 4 + [in_hbm],
        name="pedigree",
    )(parents, new_animal, sire, dam, genotypes)
    width = packed_width(traits, share)
    deviation, payload = call(
        functools.partial(deviation_kernel, share, traits, columns),
        (placed_block, shape_of(rows, PAD, width + capacity)),
        (pltpu.VMEM((PAD, LANES), F32), *chunks(chunk, KEPT)),
        in_specs=[in_vmem] * (columns + 2) + [in_hbm, in_vmem],
        name="deviation",
    )(*differences, genomic_inverse, resident, genotypes, back)
    received = exchange(payload, "rows")
    residual_table, deviation = lax.optimization_barrier((residual_table, deviation))
    table = jnp.pad(jnp.transpose(residual_table, (2, 1, 0)), ((0, 0), (0, PAD - traits), (0, 0)))
    table = table.reshape(traits * PAD, patterns)
    base_image = call(
        functools.partial(record_kernel, bits),
        animal_block,
        (
            pltpu.VMEM((PAD, LANES), F32),
            pltpu.VMEM((PAD, -(-genotyped // capacity) * capacity), F32),
        ),
        name="record",
    )(deviation, sampling, new_animal, kinds, places, table, genetic_inverse)

    if share % LANES:
        start = row[0] * share
        new_share = lax.dynamic_slice_in_dim(new_marker, start, share, 1)
        res_share = lax.dynamic_slice_in_dim(residual_marker, start, share, 1)

        def own(height):
            return pl.BlockSpec((height, share), lambda k, r: (0, 0))
    else:
        new_share, res_share = new_marker, residual_marker

        def own(height):
            return pl.BlockSpec((height, share), lambda k, r: (0, r[0]))

    def still(array):
        return pl.BlockSpec(array.shape, lambda k, r, n=len(array.shape): (0,) * n)

    out_shape = shape_of(rows, PAD, width + LANES)
    full = -(-share // LANES) * LANES
    inputs = (
        received,
        send,
        base_image,
        genetic_inverse,
        marker_inverse,
        new_animal,
        residual_animal,
    )
    image_animal, payload = pl.pallas_call(
        functools.partial(image_kernel, bits, share),
        out_shape=(animal_block, out_shape),
        grid_spec=pltpu.PrefetchScalarGridSpec(
            num_scalar_prefetch=1,
            grid=(1,),
            in_specs=[still(array) for array in inputs] + [own(PAD), own(traits)],
            out_specs=(still(animal_block), still(out_shape)),
            scratch_shapes=[
                pltpu.VMEM((PAD, LANES), F32),
                pltpu.VMEM((PAD, LANES), F32),
                pltpu.VMEM((PAD, full), F32),
                pltpu.VMEM((PAD, full), F32),
            ],
        ),
        compiler_params=LIMIT,
        name="image",
    )(row, *inputs, new_share, res_share)
    gathered = exchange(payload, "rows")
    tiles = copies_of(call(spread_kernel, tile, name="spread")(gathered), "mk")
    *outputs, reduction = call(
        functools.partial(final_kernel, share, columns),
        (
            shape_of(traits, animals),
            shape_of(traits, markers),
            shape_of(traits, animals),
            shape_of(traits, markers),
            shape_of(1, 1),
        ),
        name="final",
    )(
        sums,
        *tiles,
        solution_animal,
        residual_animal,
        new_animal,
        image_animal,
        solution_marker,
        residual_marker,
        new_marker,
        gathered,
    )
    return (*outputs, reduction.reshape(()))


def solution(mesh):
    animal, marker = P(None, ("rows", "mk")), P(None, "mk")
    index = P(("rows", "mk"))
    return jax.shard_map(
        local,
        mesh=mesh,
        in_specs=(
            animal,
            marker,
            animal,
            marker,
            animal,
            marker,
            animal,
            marker,
            P(),
            P("rows", "mk"),
            P(),
            P(),
            P(),
            P(),
            index,
            index,
            index,
            index,
            P("rows", "mk", None, None),
        ),
        out_specs=(animal, marker, animal, marker, P()),
        check_vma=False,
    )
```
